128 devices in a mesh: grp: 2 (over core), pts: 64 (over z, x, y).
Axes of the slice: x: 4, y: 4, z: 4, core: 2. Of those that a mesh axis runs over, the one named last changes fastest.
Arguments:
- element_attribute_table: bfloat16 [1048576, 512], P(('grp', 'pts')), parts along dimension 0, may hold values from -16 to 16
- active_group_tally: int32 [128], P(('grp', 'pts')), parts along dimension 0, may hold values from 48 to 64, as said below
- group_destination_part: int32 [8192], P(('grp', 'pts')), parts along dimension 0, may hold values from 0 to 63, as said below
- element_vertex_permutation: int32 [8192, 128], P(('grp', 'pts')), parts along dimension 0, may hold values from 0 to 127, each once within a row
- softness_factor: float32 [8], replicated, may hold values from 0.15 to 0.6
- entry_projection_coefficients: bfloat16 [512, 1024], replicated, may hold values from -0.25 to 0.25
- partition_score_coefficients: bfloat16 [8, 64, 256], replicated, may hold values from -0.75 to 0.75
- summary_query_key_coefficients: bfloat16 [64, 192], replicated, may hold values from -0.75 to 0.75
- final_projection_coefficients: bfloat16 [512, 512], replicated, may hold values from -0.25 to 0.25
Outputs:
- point_features: bfloat16 [1048576, 512], P(('grp', 'pts')), parts along dimension 0
The draws below stay inside these ranges and needn't reach their ends.
There are 2 independent parts, one for each index of `grp`. The reference program is written for one: setup_inputs(seed, part) draws one part's arguments, and reference() takes and returns one part's arrays. A program takes and returns all parts, laid end to end along the dimension named above; an argument that names none is the same for every part. Nothing has to cross between parts.
Inputs may be any that keep to these rules, and one draw needn't show every extreme that they name: The live blocks of a device are its first active_group_tally slots; some device has all 64 live. `group_destination_part`: no device names a point shard in more than 1 of its slots; some point shard is named exactly 1 times by the live blocks of every device. `element_vertex_permutation`: each row is a permutation.
All inputs are finite; a program needn't handle non-finite values.
Results may differ from the reference program's by a relative error of at most 0.0016.
Values may be sent and summed in bfloat16 or wider, within the bound.
A program may use at most 192 MiB of HBM per device.

```python
import math
import jax
import jax.numpy as jnp
from jax import lax

C = 512
ATTENDER_AMOUNT = 8
S = 256
BLOCK = 128
BLK_DEV = 64
HD = 64
CAP = 1
NB = 4096
NCELL = 524288
N_PTS = 64


def draw_active_group_tally(key, part):
    least = BLK_DEV - BLK_DEV // 4
    counts = jax.random.randint(jax.random.fold_in(key, 21), (N_PTS,), least, BLK_DEV + 1)
    fullest = jax.random.randint(jax.random.fold_in(key, 22), (), 0, N_PTS)
    return jnp.where(jnp.arange(N_PTS) == fullest, BLK_DEV, counts).astype(jnp.int32)


def draw_group_destination_part(key, part):
    least = BLK_DEV - BLK_DEV // 4
    others_total = (N_PTS - 1) * CAP
    target = jax.random.randint(jax.random.fold_in(key, 11), (), 0, N_PTS)

    def one_device(device_key):
        first_key, second_key = jax.random.split(device_key)
        others = jnp.arange(others_total, dtype=jnp.int32) // CAP
        others = others + (others >= target).astype(jnp.int32)
        others = others[jax.random.permutation(first_key, others_total)]
        other_scores = 2 * jnp.arange(others_total, dtype=jnp.int32) + 1
        places = jax.random.permutation(second_key, least - CAP + 1)[:CAP].astype(jnp.int32)
        target_scores = 2 * places
        values = jnp.concatenate([others, jnp.full((CAP,), target, jnp.int32)])
        scores = jnp.concatenate([other_scores, target_scores])
        order = jnp.argsort(scores, stable=True)
        return values[order][:BLK_DEV]
    device_keys = jax.random.split(jax.random.fold_in(key, 12), N_PTS)
    return jax.vmap(one_device)(device_keys).reshape(-1).astype(jnp.int32)


def strengthened(entries, own_key, source, target, blocks, factor):
    owner, partner = [(jnp.arange(entries.shape[position]) // (entries.shape[position] // blocks)).reshape([-1 if axis == position else 1 for axis in range(entries.ndim)]) for position in (source, target)]
    chosen = jax.random.permutation(own_key, blocks)[partner]
    strong = (owner == chosen) | (owner == (partner + blocks // 2) % blocks)
    return jnp.where(strong, factor * entries, entries)


def steps_of(rng, shape, cuts, smallest, largest):
    level = 1.0
    for axis_at, blocks in cuts:
        draws = jax.random.uniform(jax.random.fold_in(jax.random.fold_in(rng, 6), axis_at), (blocks,), jnp.float32, smallest / len(cuts), largest / len(cuts))
        level = level * jnp.repeat(jnp.exp(draws), shape[axis_at] // blocks).reshape((-1,) + (1,) * (len(shape) - 1 - axis_at))
    return level


def scatter_about(stream_key, extent, deviation, most, cuts=(), kind=jnp.bfloat16):
    array = deviation * jax.random.normal(stream_key, extent, jnp.float32)
    if cuts:
        array = array * steps_of(stream_key, extent, cuts, -0.22, 0.18)
    return jnp.clip(array, -most, most).astype(kind)


def bell_draw_with(own_key, extent, scale, reach, cuts, heavy, kind=jnp.bfloat16):
    result = scale * jax.random.normal(own_key, extent, jnp.float32)
    if cuts:
        result = result * steps_of(own_key, extent, cuts, -0.22, 0.18)
    return jnp.clip(strengthened(result, jax.random.fold_in(own_key, 3), *heavy), -reach, reach).astype(kind)


def setup_inputs(seed: int = 0, part: int = 0) -> dict:
    key_of = jax.random.split(jax.random.key(seed), 10)
    part_splits = jax.random.split(jax.random.fold_in(key_of[9], part), 10)
    return {
        "element_attribute_table": bell_draw_with(part_splits[0], (NCELL, C), 1.0, 16.0, ((0, 64),), (0, 1, 64, 4.0)),
        "active_group_tally": draw_active_group_tally(jax.random.fold_in(jax.random.fold_in(key_of[9], part), 71), part),
        "group_destination_part": draw_group_destination_part(jax.random.fold_in(jax.random.fold_in(key_of[9], part), 71), part),
        "element_vertex_permutation": jax.vmap(lambda own: jax.random.permutation(own, BLOCK))(jax.random.split(part_splits[3], NB)).reshape((NB, BLOCK)).astype(jnp.int32),
        "softness_factor": jnp.clip(jnp.exp(jax.random.uniform(key_of[4], (ATTENDER_AMOUNT,), jnp.float32, math.log(0.15), math.log(0.6))), 0.15, 0.6),
        "entry_projection_coefficients": scatter_about(key_of[5], (C, 2 * C), C ** -0.5, 0.25),
        "partition_score_coefficients": scatter_about(key_of[6], (ATTENDER_AMOUNT, HD, S), HD ** -0.5, 0.75),
        "summary_query_key_coefficients": scatter_about(key_of[7], (HD, 3 * HD), HD ** -0.5, 0.75),
        "final_projection_coefficients": scatter_about(key_of[8], (C, C), C ** -0.5, 0.25),
    }


NORM_EPS = 1e-05
SLICE_EPS = 1e-05

def normalize_rows(point_rows):
    values = point_rows.astype(jnp.float32)
    centre = lax.optimization_barrier(jnp.mean(values, axis=-1, keepdims=True))
    spread = lax.optimization_barrier(jnp.mean(jnp.square(values - centre), axis=-1, keepdims=True))
    return ((values - centre) * lax.rsqrt(spread + NORM_EPS)).astype(jnp.bfloat16)

def slice_attention(tokens, summary_query_key_coefficients):
    head_width = tokens.shape[-1]
    project = jnp.einsum('hsd,de->hse', tokens, summary_query_key_coefficients.astype(jnp.float32), precision=lax.Precision.HIGHEST)
    queries = project[..., :head_width]
    slice_keys = project[..., head_width:2 * head_width]
    slice_values = project[..., 2 * head_width:]
    scores = jnp.einsum('hsd,htd->hst', queries, slice_keys, precision=lax.Precision.HIGHEST) * head_width ** (-0.5)
    powered_entries = jnp.exp(scores)
    attend = powered_entries / lax.optimization_barrier(jnp.sum(powered_entries, axis=-1, keepdims=True))
    return jnp.einsum('hst,htd->hsd', attend, slice_values, precision=lax.Precision.HIGHEST).astype(jnp.bfloat16)

def reference(element_attribute_table, active_group_tally, group_destination_part, element_vertex_permutation, softness_factor, entry_projection_coefficients, partition_score_coefficients, summary_query_key_coefficients, final_projection_coefficients):
    block_total = N_PTS * BLK_DEV
    blocks = jnp.take_along_axis(element_attribute_table.reshape(block_total, BLOCK, C), element_vertex_permutation[:, :, None].astype(jnp.int32), axis=1)
    positions = jnp.arange(BLK_DEV, dtype=jnp.int32)
    block_live = positions[None, :] < active_group_tally[:, None]
    device_rows = blocks.reshape(N_PTS, BLK_DEV * BLOCK, C)
    row_live = jnp.repeat(block_live.astype(jnp.float32), BLOCK, axis=1)

    def slice_weights(point_rows):
        mixed = jnp.dot(normalize_rows(point_rows), entry_projection_coefficients, preferred_element_type=jnp.float32)
        feature_matrix = mixed[:, :C].astype(jnp.bfloat16)
        middle_result = mixed[:, C:].astype(jnp.bfloat16)
        partition_raw_scores = jnp.einsum('rhd,hds->rhs', middle_result.reshape(-1, ATTENDER_AMOUNT, HD).astype(jnp.float32), partition_score_coefficients.astype(jnp.float32))
        partition_raw_scores = partition_raw_scores / softness_factor[None, :, None]
        powered_entries = jnp.exp(partition_raw_scores)
        weights = (powered_entries / lax.optimization_barrier(jnp.sum(powered_entries, axis=-1, keepdims=True))).astype(jnp.bfloat16)
        return (feature_matrix, weights)

    def accumulate(carry, item):
        point_rows, live_mask = item
        feature_matrix, weights = slice_weights(point_rows)
        masked = weights * live_mask[:, None, None].astype(jnp.bfloat16)
        numer = jnp.einsum('rhs,rhd->hsd', masked.astype(jnp.float32), feature_matrix.reshape(-1, ATTENDER_AMOUNT, HD).astype(jnp.float32))
        denom = lax.optimization_barrier(jnp.sum(masked.astype(jnp.float32), axis=0))
        return ((carry[0] + numer, carry[1] + denom), None)
    start = (jnp.zeros((ATTENDER_AMOUNT, S, HD), jnp.float32), jnp.zeros((ATTENDER_AMOUNT, S), jnp.float32))
    (numer, denom), _ = lax.scan(accumulate, start, (device_rows, row_live))
    tokens = numer / (denom[..., None] + SLICE_EPS)
    mixed_tokens = slice_attention(tokens, summary_query_key_coefficients)

    def finish(item):
        point_rows, live_mask = item
        feature_matrix, weights = slice_weights(point_rows)
        spread_back = jnp.einsum('rhs,hsd->rhd', weights.astype(jnp.float32), mixed_tokens.astype(jnp.float32))
        spread_back = spread_back.astype(jnp.bfloat16).reshape(-1, C)
        update = jnp.dot(spread_back, final_projection_coefficients, preferred_element_type=jnp.float32)
        return ((point_rows.astype(jnp.float32) + update) * live_mask[:, None]).astype(jnp.bfloat16)
    results = lax.map(finish, (device_rows, row_live))
    block_results = results.reshape(block_total, BLOCK, C)
    dest_table = group_destination_part.reshape(N_PTS, BLK_DEV).astype(jnp.int32)
    earlier = (dest_table[:, :, None] == dest_table[:, None, :]) & (positions[None, None, :] < positions[None, :, None])
    rank = lax.optimization_barrier(jnp.sum(earlier.astype(jnp.int32), axis=2))
    owners = jnp.arange(N_PTS, dtype=jnp.int32)[:, None]
    target = dest_table * (N_PTS * CAP) + owners * CAP + rank
    dummy = N_PTS * N_PTS * CAP
    target = jnp.where(block_live, target, dummy).reshape(-1).astype(jnp.int32)
    placed = jnp.zeros((dummy + 1, BLOCK, C), jnp.bfloat16).at[target].set(block_results)
    return placed[:dummy].reshape(-1, C)
```

```python
import functools

import jax
import jax.numpy as jnp
from jax import lax
from jax.experimental import pallas as pl
from jax.experimental.pallas import tpu as pltpu
from jax.sharding import PartitionSpec as P

F32 = jnp.float32
BF16 = jnp.bfloat16
MESH = pl.DeviceIdType.MESH
LOG2E = 1.4426950408889634
NORM_EPS = 1e-05
SLICE_EPS = 1e-05
HIGHEST = lax.Precision.HIGHEST
NT = (((1,), (1,)), ((), ()))
TN = (((0,), (0,)), ((), ()))

C = 512
HEADS = 8
S = 256
HD = 64
BLOCK = 128
BLOCKS = 64
PEERS = 64
SIDE = 4
STEP_ROWS = 1024
STEP_BLOCKS = STEP_ROWS // BLOCK
STEPS = BLOCKS * BLOCK // STEP_ROWS
ACC_ROWS = HD + 16
MSG_ROWS = 24
VMEM_LIMIT = 60 << 20


def whole(shape):
    return pl.BlockSpec(shape, lambda *_: (0,) * len(shape))


def normalize_rows(rows):
    values = rows.astype(F32)
    centred = values - jnp.mean(values, axis=-1, keepdims=True)
    spread = jnp.mean(centred * centred, axis=-1, keepdims=True)
    return (centred * lax.rsqrt(spread + NORM_EPS)).astype(BF16)


def head_weights(middle, score_ref, scale_ref, head):
    pair = middle[:, (head // 2) * 128 : (head // 2) * 128 + 128]
    scores = jnp.dot(pair, score_ref[head], preferred_element_type=F32)
    powered = jnp.exp2(scores * scale_ref[head])
    return (powered * (1.0 / jnp.sum(powered, axis=-1, keepdims=True))).astype(BF16)


def place_kernel(source_ref, table_ref, order_ref, placed_ref):
    rows = lax.broadcasted_iota(jnp.int32, (BLOCK, BLOCK), 0)

    @pl.loop(0, PEERS)
    def _(p):
        b = source_ref[p]
        picking = (order_ref[pl.ds(b, 1), :] == rows).astype(F32).astype(BF16)
        placed_ref[p] = lax.dot_general(
            picking, table_ref[b], TN, preferred_element_type=F32
        ).astype(BF16)


def place(source, table, order):
    return pl.pallas_call(
        place_kernel,
        name="place",
        out_shape=jax.ShapeDtypeStruct((PEERS, BLOCK, C), BF16),
        in_specs=[
            pl.BlockSpec(memory_space=pltpu.SMEM),
            pl.BlockSpec(memory_space=pltpu.VMEM),
            pl.BlockSpec(memory_space=pltpu.VMEM),
        ],
        out_specs=pl.BlockSpec(memory_space=pltpu.VMEM),
        compiler_params=pltpu.CompilerParams(vmem_limit_bytes=VMEM_LIMIT),
    )(source, table, order)


def sums_kernel(
    tally_ref, scale_ref, flag_ref, table_ref, feature_ref, middle_ref, score_ref, msg_ref, acc_ref
):
    step = pl.program_id(0)

    @pl.when(step == 0)
    def _():
        acc_ref[...] = jnp.zeros_like(acc_ref)

    normed = normalize_rows(table_ref[...])
    live = (
        lax.broadcasted_iota(jnp.int32, (1, STEP_ROWS), 1)
        < (tally_ref[0] - step * STEP_BLOCKS) * BLOCK
    ).astype(F32)
    features = lax.dot_general(feature_ref[...], normed, NT, preferred_element_type=F32)
    features = (features * live).astype(BF16)
    ones = jnp.broadcast_to(live, (16, STEP_ROWS)).astype(BF16)
    middle = jnp.dot(normed, middle_ref[...], preferred_element_type=F32).astype(BF16)
    for head in range(HEADS):
        weights = head_weights(middle, score_ref, scale_ref, head)
        left = jnp.concatenate([features[head * HD : head * HD + HD], ones], axis=0)
        acc_ref[head] += jnp.dot(left, weights, preferred_element_type=F32)

    @pl.when(step == pl.num_programs(0) - 1)
    def _():
        for p in range(PEERS):
            head, part = p // 8, (p % 8) * 8
            msg_ref[p, 0:8, :] = acc_ref[head, part : part + 8, 0:128]
            msg_ref[p, 8:16, :] = acc_ref[head, part : part + 8, 128:256]
            msg_ref[p, 16:17, :] = acc_ref[head, HD : HD + 1, 0:128]
            msg_ref[p, 17:18, :] = acc_ref[head, HD : HD + 1, 128:256]
        msg_ref[:, 18:24, :] = flag_ref[:, 0:6, :]


def partial_sums(tally, scale, flags, table, feature, middle, score):
    return pl.pallas_call(
        sums_kernel,
        name="partial_sums",
        grid=(STEPS,),
        out_shape=jax.ShapeDtypeStruct((PEERS, MSG_ROWS, 128), F32),
        in_specs=[
            pl.BlockSpec(memory_space=pltpu.SMEM),
            pl.BlockSpec(memory_space=pltpu.SMEM),
            whole((PEERS, 8, 128)),
            pl.BlockSpec((STEP_ROWS, C), lambda i: (i, 0)),
            whole((C, C)),
            whole((C, C)),
            whole((HEADS, 128, S)),
        ],
        out_specs=whole((PEERS, MSG_ROWS, 128)),
        scratch_shapes=[pltpu.VMEM((HEADS, ACC_ROWS, S), F32)],
        compiler_params=pltpu.CompilerParams(vmem_limit_bytes=VMEM_LIMIT),
        cost_estimate=pl.CostEstimate(
            flops=40_000_000_000, bytes_accessed=10_000_000, transcendentals=17_000_000
        ),
    )(tally, scale, flags, table, feature, middle, score)


def peer_at(me, r, sign):
    z, x, y = me // 16, (me // 4) % 4, me % 4
    dz, dx, dy = r // 16, (r // 4) % 4, r % 4
    return (
        ((z + sign * dz + SIDE) % SIDE) * 16
        + ((x + sign * dx + SIDE) % SIDE) * 4
        + (y + sign * dy + SIDE) % SIDE
    )


def reduce_kernel(
    msg_ref, tokens_ref, flags_ref, got_ref, mine_ref, send_sem, recv_sem, back_send, back_recv
):
    me = lax.axis_index("pts")
    barrier = pltpu.get_barrier_semaphore()

    @pl.loop(1, PEERS)
    def _(r):
        pl.semaphore_signal(
            barrier, inc=1, device_id={"pts": peer_at(me, r, 1)}, device_id_type=MESH
        )

    pl.semaphore_wait(barrier, PEERS - 1)

    def there(r):
        p = peer_at(me, r, 1)
        return pltpu.make_async_remote_copy(
            src_ref=msg_ref.at[p],
            dst_ref=got_ref.at[me],
            send_sem=send_sem.at[r],
            recv_sem=recv_sem.at[me],
            device_id={"pts": p},
            device_id_type=MESH,
        )

    def arriving(r):
        p = peer_at(me, r, -1)
        return pltpu.make_async_remote_copy(
            src_ref=msg_ref.at[p],
            dst_ref=got_ref.at[p],
            send_sem=send_sem.at[r],
            recv_sem=recv_sem.at[p],
            device_id={"pts": p},
            device_id_type=MESH,
        )

    @pl.loop(1, PEERS)
    def _(r):
        there(r).start()

    got_ref[me] = msg_ref[me]

    @pl.loop(1, PEERS)
    def _(r):
        arriving(r).wait_recv()

    total = lax.fori_loop(
        0, PEERS, lambda s, t: t + got_ref[s], jnp.zeros((MSG_ROWS, 128), F32)
    )
    mine_ref[0:8, :] = total[0:8] / (total[16:17] + SLICE_EPS)
    mine_ref[8:16, :] = total[8:16] / (total[17:18] + SLICE_EPS)

    def back(r):
        p = peer_at(me, r, 1)
        return pltpu.make_async_remote_copy(
            src_ref=mine_ref,
            dst_ref=tokens_ref.at[me],
            send_sem=back_send.at[r],
            recv_sem=back_recv.at[me],
            device_id={"pts": p},
            device_id_type=MESH,
        )

    def returning(r):
        p = peer_at(me, r, -1)
        return pltpu.make_async_remote_copy(
            src_ref=mine_ref,
            dst_ref=tokens_ref.at[p],
            send_sem=back_send.at[r],
            recv_sem=back_recv.at[p],
            device_id={"pts": p},
            device_id_type=MESH,
        )

    @pl.loop(1, PEERS)
    def _(r):
        back(r).start()

    flags_ref[...] = got_ref[:, 16:24, :]
    tokens_ref[me] = mine_ref[...]

    @pl.loop(1, PEERS)
    def _(r):
        returning(r).wait_recv()

    @pl.loop(1, PEERS)
    def _(r):
        there(r).wait_send()
        back(r).wait_send()


def reduce_tokens(msg):
    return pl.pallas_call(
        reduce_kernel,
        name="reduce_tokens",
        out_shape=(
            jax.ShapeDtypeStruct((PEERS, 16, 128), F32),
            jax.ShapeDtypeStruct((PEERS, 8, 128), F32),
        ),
        in_specs=[pl.BlockSpec(memory_space=pltpu.VMEM)],
        out_specs=[pl.BlockSpec(memory_space=pltpu.VMEM)] * 2,
        scratch_shapes=[
            pltpu.VMEM((PEERS, MSG_ROWS, 128), F32),
            pltpu.VMEM((16, 128), F32),
            pltpu.SemaphoreType.DMA((PEERS,)),
            pltpu.SemaphoreType.DMA((PEERS,)),
            pltpu.SemaphoreType.DMA((PEERS,)),
            pltpu.SemaphoreType.DMA((PEERS,)),
        ],
        compiler_params=pltpu.CompilerParams(
            collective_id=1, has_side_effects=True, vmem_limit_bytes=VMEM_LIMIT
        ),
        cost_estimate=pl.CostEstimate(
            flops=1_000_000, bytes_accessed=60_000_000, transcendentals=0
        ),
    )(msg)


def mix_tokens(tokens_ref, qkv_ref, mixed_ref):
    for head in range(HEADS):
        tokens = jnp.concatenate(
            [
                jnp.concatenate(
                    [tokens_ref[head * 8 + j, 0:8, :], tokens_ref[head * 8 + j, 8:16, :]], axis=1
                )
                for j in range(8)
            ],
            axis=0,
        )
        project = jnp.dot(qkv_ref[...], tokens, preferred_element_type=F32, precision=HIGHEST)
        queries = jnp.transpose(project[0:HD])
        scores = jnp.dot(
            queries, project[HD : 2 * HD], preferred_element_type=F32, precision=HIGHEST
        ) * (HD**-0.5)
        powered = jnp.exp(scores)
        attend = powered / jnp.sum(powered, axis=-1, keepdims=True)
        mixed = lax.dot_general(
            attend, project[2 * HD :], NT, preferred_element_type=F32, precision=HIGHEST
        )
        zeros = jnp.zeros_like(mixed)
        padded = [mixed, zeros] if head % 2 == 0 else [zeros, mixed]
        mixed_ref[head] = jnp.concatenate(padded, axis=1).astype(BF16)


def finish_kernel(
    scale_ref,
    tokens_ref,
    flags_ref,
    qkv_ref,
    rows_ref,
    middle_ref,
    score_ref,
    final_ref,
    out_ref,
    mixed_ref,
):
    step = pl.program_id(0)

    @pl.when(step == 0)
    def _():
        mix_tokens(tokens_ref, qkv_ref, mixed_ref)

    rows = rows_ref[...]
    middle = jnp.dot(
        normalize_rows(rows), middle_ref[...], preferred_element_type=F32
    ).astype(BF16)
    spread = []
    for pair in range(HEADS // 2):
        first = head_weights(middle, score_ref, scale_ref, 2 * pair)
        second = head_weights(middle, score_ref, scale_ref, 2 * pair + 1)
        spread.append(
            (
                jnp.dot(first, mixed_ref[2 * pair], preferred_element_type=F32)
                + jnp.dot(second, mixed_ref[2 * pair + 1], preferred_element_type=F32)
            ).astype(BF16)
        )
    spread = jnp.concatenate(spread, axis=1)
    update = jnp.dot(spread, final_ref[...], preferred_element_type=F32)
    for b in range(STEP_BLOCKS):
        flag = flags_ref[step * STEP_BLOCKS + b, 2:3, :]
        flag = jnp.concatenate([flag] * (C // 128), axis=1)
        part = slice(b * BLOCK, (b + 1) * BLOCK)
        out_ref[part, :] = ((rows[part].astype(F32) + update[part]) * flag).astype(BF16)


def finish(scale, tokens, flags, qkv, rows, middle, score, final):
    return pl.pallas_call(
        finish_kernel,
        name="finish",
        grid=(STEPS,),
        out_shape=jax.ShapeDtypeStruct((BLOCKS * BLOCK, C), BF16),
        in_specs=[
            pl.BlockSpec(memory_space=pltpu.SMEM),
            whole((PEERS, 16, 128)),
            whole((PEERS, 8, 128)),
            whole((3 * HD, HD)),
            pl.BlockSpec((STEP_ROWS, C), lambda i: (i, 0)),
            whole((C, C)),
            whole((HEADS, 128, S)),
            whole((C, C)),
        ],
        out_specs=pl.BlockSpec((STEP_ROWS, C), lambda i: (i, 0)),
        scratch_shapes=[pltpu.VMEM((HEADS, S, 128), BF16)],
        compiler_params=pltpu.CompilerParams(vmem_limit_bytes=VMEM_LIMIT),
        cost_estimate=pl.CostEstimate(
            flops=30_000_000_000, bytes_accessed=20_000_000, transcendentals=17_000_000
        ),
    )(scale, tokens, flags, qkv, rows, middle, score, final)


def per_device(table, tally, destination, order, softness, entry, score, qkv, final):
    slots = jnp.arange(BLOCKS, dtype=jnp.int32)
    hit = (destination[None, :] == slots[:, None]) & (slots[None, :] < tally[0])
    source = jnp.sum(jnp.where(hit, slots[None, :], 0), axis=1)
    flags = jnp.broadcast_to(
        jnp.sum(hit.astype(F32), axis=1)[:, None, None], (PEERS, 8, 128)
    )
    scale = LOG2E / softness
    empty = jnp.zeros((HEADS // 2, HD, S), BF16)
    score = jnp.stack(
        [
            jnp.concatenate([score[0::2], empty], axis=1),
            jnp.concatenate([empty, score[1::2]], axis=1),
        ],
        axis=1,
    ).reshape(HEADS, 2 * HD, S)
    feature = jnp.transpose(entry[:, :C])
    middle = entry[:, C:]
    qkv = jnp.transpose(qkv).astype(F32)

    placed = place(source, table.reshape(BLOCKS, BLOCK, C), order)
    arrived = lax.all_to_all(placed, "pts", split_axis=0, concat_axis=0, tiled=True)
    msg = partial_sums(tally, scale, flags, table, feature, middle, score)
    tokens, flags = reduce_tokens(msg)
    return finish(
        scale, tokens, flags, qkv, arrived.reshape(BLOCKS * BLOCK, C), middle, score, final
    )


def solution(mesh):
    split = P(("grp", "pts"))
    rows = P(("grp", "pts"), None)
    return jax.shard_map(
        per_device,
        mesh=mesh,
        in_specs=(rows, split, split, rows, P(), P(), P(), P(), P()),
        out_specs=rows,
        check_vma=False,
    )
```

```python
import functools

import jax
import jax.numpy as jnp
from jax import lax
from jax.experimental import pallas as pl
from jax.experimental.pallas import tpu as pltpu
from jax.sharding import PartitionSpec as P

F32 = jnp.float32
BF16 = jnp.bfloat16
MESH = pl.DeviceIdType.MESH
LOG2E = 1.4426950408889634
NORM_EPS = 1e-05
SLICE_EPS = 1e-05
HIGHEST = lax.Precision.HIGHEST
NT = (((1,), (1,)), ((), ()))
TN = (((0,), (0,)), ((), ()))

C = 512
HEADS = 8
S = 256
HD = 64
BLOCK = 128
BLOCKS = 64
PEERS = 64
SIDE = 4
STEP_ROWS = 1024
STEP_BLOCKS = STEP_ROWS // BLOCK
STEPS = BLOCKS * BLOCK // STEP_ROWS
ACC_ROWS = HD + 16
MSG_ROWS = 24
VMEM_LIMIT = 60 << 20
SEND_STEP = 4
SEND_REDUCE = 10


def whole(shape):
    return pl.BlockSpec(shape, lambda *_: (0,) * len(shape))


def normalize_rows(rows):
    values = rows.astype(F32)
    centred = values - jnp.mean(values, axis=-1, keepdims=True)
    spread = jnp.mean(centred * centred, axis=-1, keepdims=True)
    return (centred * lax.rsqrt(spread + NORM_EPS)).astype(BF16)


def head_weights(middle, score_ref, scale_ref, head):
    pair = middle[:, (head // 2) * 128 : (head // 2) * 128 + 128]
    scores = jnp.dot(pair, score_ref[head], preferred_element_type=F32)
    powered = jnp.exp2(scores * scale_ref[head])
    return (powered * (1.0 / jnp.sum(powered, axis=-1, keepdims=True))).astype(BF16)


def mix_tokens(tokens_ref, qkv_ref, mixed_ref):
    for head in range(HEADS):
        tokens = jnp.concatenate(
            [
                jnp.concatenate(
                    [tokens_ref[head * 8 + j, 0:8, :], tokens_ref[head * 8 + j, 8:16, :]], axis=1
                )
                for j in range(8)
            ],
            axis=0,
        )
        project = jnp.dot(qkv_ref[...], tokens, preferred_element_type=F32, precision=HIGHEST)
        queries = jnp.transpose(project[0:HD])
        scores = jnp.dot(
            queries, project[HD : 2 * HD], preferred_element_type=F32, precision=HIGHEST
        ) * (HD**-0.5)
        powered = jnp.exp(scores)
        attend = powered / jnp.sum(powered, axis=-1, keepdims=True)
        mixed = lax.dot_general(
            attend, project[2 * HD :], NT, preferred_element_type=F32, precision=HIGHEST
        )
        zeros = jnp.zeros_like(mixed)
        padded = [mixed, zeros] if head % 2 == 0 else [zeros, mixed]
        mixed_ref[head] = jnp.concatenate(padded, axis=1).astype(BF16)


def peer_at(me, i, sign):
    z, x, y = me // 16, (me // 4) % 4, me % 4
    a, b, c = i % 4, (i // 4) % 4, i // 16
    return (
        ((z + sign * a + 8) % SIDE) * 16
        + ((x + sign * (a + b) + 8) % SIDE) * 4
        + (y + sign * (a + c) + 8) % SIDE
    )


def layer_kernel(
    source_ref,
    tally_ref,
    scale_ref,
    table_hbm,
    order_ref,
    flag_ref,
    feature_ref,
    middle_ref,
    score_ref,
    qkv_ref,
    final_ref,
    out_hbm,
    table_ref,
    outgoing_ref,
    arrived_ref,
    done_ref,
    acc_ref,
    msg_ref,
    got_ref,
    mine_ref,
    tokens_ref,
    mixed_ref,
    load_sem,
    store_sem,
    block_send,
    block_recv,
    sum_send,
    sum_recv,
    token_send,
    token_recv,
):
    me = lax.axis_index("pts")
    barrier = pltpu.get_barrier_semaphore()
    load = pltpu.make_async_copy(table_hbm, table_ref, load_sem)
    load.start()

    @pl.loop(1, PEERS)
    def _(i):
        pl.semaphore_signal(
            barrier, inc=1, device_id={"pts": peer_at(me, i, 1)}, device_id_type=MESH
        )

    def copy(src, dst, send, recv, i):
        return pltpu.make_async_remote_copy(
            src_ref=src,
            dst_ref=dst,
            send_sem=send.at[i],
            recv_sem=recv.at[i],
            device_id={"pts": peer_at(me, i, 1)},
            device_id_type=MESH,
        )

    def block_copy(i):
        return copy(outgoing_ref.at[i], arrived_ref.at[i], block_send, block_recv, i)

    def sum_copy(i):
        return copy(msg_ref.at[peer_at(me, i, 1)], got_ref.at[i], sum_send, sum_recv, i)

    def token_copy(i):
        return copy(mine_ref, tokens_ref.at[me], token_send, token_recv, i)

    def token_arrival(i):
        return copy(mine_ref, tokens_ref.at[peer_at(me, i, -1)], token_send, token_recv, i)

    rows = lax.broadcasted_iota(jnp.int32, (BLOCK, BLOCK), 0)

    def placed(i):
        b = source_ref[peer_at(me, i, 1)]
        picking = (order_ref[b] == rows).astype(F32).astype(BF16)
        return lax.dot_general(picking, table_ref[b], TN, preferred_element_type=F32).astype(
            BF16
        )

    def place(first, count):
        for j in range(count):
            outgoing_ref[first + j] = placed(first + j)

    def send(first, count):
        @pl.loop(first, first + count)
        def _(i):
            block_copy(i).start()

    load.wait()
    place(1, SEND_STEP)
    pl.semaphore_wait(barrier, PEERS - 1)
    acc_ref[...] = jnp.zeros_like(acc_ref)

    @pl.loop(0, STEPS)
    def _(step):
        first = 1 + step * SEND_STEP
        send(first, SEND_STEP)
        place(first + SEND_STEP, SEND_STEP)
        part = table_ref[pl.ds(step * STEP_BLOCKS, STEP_BLOCKS)].reshape(STEP_ROWS, C)
        normed = normalize_rows(part)
        live = (
            lax.broadcasted_iota(jnp.int32, (1, STEP_ROWS), 1)
            < (tally_ref[0] - step * STEP_BLOCKS) * BLOCK
        ).astype(F32)
        features = lax.dot_general(feature_ref[...], normed, NT, preferred_element_type=F32)
        features = (features * live).astype(BF16)
        ones = jnp.broadcast_to(live, (16, STEP_ROWS)).astype(BF16)
        middle = jnp.dot(normed, middle_ref[...], preferred_element_type=F32).astype(BF16)
        for head in range(HEADS):
            weights = head_weights(middle, score_ref, scale_ref, head)
            left = jnp.concatenate([features[head * HD : head * HD + HD], ones], axis=0)
            acc_ref[head] += jnp.dot(left, weights, preferred_element_type=F32)

    for p in range(PEERS):
        head, part = p // 8, (p % 8) * 8
        msg_ref[p, 0:8, :] = acc_ref[head, part : part + 8, 0:128]
        msg_ref[p, 8:16, :] = acc_ref[head, part : part + 8, 128:256]
        msg_ref[p, 16:17, :] = acc_ref[head, HD : HD + 1, 0:128]
        msg_ref[p, 17:18, :] = acc_ref[head, HD : HD + 1, 128:256]
    msg_ref[:, 18:24, :] = flag_ref[:, 0:6, :]

    sent = 1 + STEPS * SEND_STEP
    ready = sent + SEND_STEP
    arrived_ref[0] = placed(0)

    @pl.loop(ready, PEERS)
    def _(i):
        outgoing_ref[i] = placed(i)

    @pl.loop(1, PEERS)
    def _(i):
        sum_copy(i).start()

    send(sent, SEND_REDUCE)
    got_ref[0] = msg_ref[me]

    def add(i, total):
        sum_copy(i).wait_recv()
        return total + got_ref[i]

    total = lax.fori_loop(1, PEERS, add, got_ref[0])
    mine_ref[0:8, :] = total[0:8] / (total[16:17] + SLICE_EPS)
    mine_ref[8:16, :] = total[8:16] / (total[17:18] + SLICE_EPS)
    tokens_ref[me] = mine_ref[...]

    @pl.loop(1, PEERS)
    def _(i):
        token_copy(i).start()

    send(sent + SEND_REDUCE, PEERS - sent - SEND_REDUCE)

    @pl.loop(1, PEERS)
    def _(i):
        token_arrival(i).wait_recv()

    mix_tokens(tokens_ref, qkv_ref, mixed_ref)

    def store(step, j):
        slot = step % 2
        return pltpu.make_async_copy(
            done_ref.at[slot, j],
            out_hbm.at[peer_at(me, step * STEP_BLOCKS + j, -1)],
            store_sem.at[slot, j],
        )

    @pl.loop(0, STEPS)
    def _(step):
        for j in range(STEP_BLOCKS):
            i = step * STEP_BLOCKS + j

            @pl.when(i > 0)
            def _():
                block_copy(i).wait_recv()

        @pl.when(step >= 2)
        def _():
            for j in range(STEP_BLOCKS):
                store(step - 2, j).wait()

        block_rows = arrived_ref[pl.ds(step * STEP_BLOCKS, STEP_BLOCKS)].reshape(STEP_ROWS, C)
        middle = jnp.dot(
            normalize_rows(block_rows), middle_ref[...], preferred_element_type=F32
        ).astype(BF16)
        spread = []
        for pair in range(HEADS // 2):
            first = head_weights(middle, score_ref, scale_ref, 2 * pair)
            second = head_weights(middle, score_ref, scale_ref, 2 * pair + 1)
            spread.append(
                (
                    jnp.dot(first, mixed_ref[2 * pair], preferred_element_type=F32)
                    + jnp.dot(second, mixed_ref[2 * pair + 1], preferred_element_type=F32)
                ).astype(BF16)
            )
        spread = jnp.concatenate(spread, axis=1)
        update = jnp.dot(spread, final_ref[...], preferred_element_type=F32)
        for j in range(STEP_BLOCKS):
            flag = got_ref[step * STEP_BLOCKS + j, 18:19, :]
            flag = jnp.concatenate([flag] * (C // 128), axis=1)
            part = slice(j * BLOCK, (j + 1) * BLOCK)
            done_ref[step % 2, j] = (
                (block_rows[part].astype(F32) + update[part]) * flag
            ).astype(BF16)
        for j in range(STEP_BLOCKS):
            store(step, j).start()

    for step in (STEPS - 2, STEPS - 1):
        for j in range(STEP_BLOCKS):
            store(step, j).wait()

    @pl.loop(1, PEERS)
    def _(i):
        block_copy(i).wait_send()
        sum_copy(i).wait_send()
        token_copy(i).wait_send()


def layer(source, tally, scale, table, order, flags, feature, middle, score, qkv, final):
    smem = pl.BlockSpec(memory_space=pltpu.SMEM)
    vmem = pl.BlockSpec(memory_space=pltpu.VMEM)
    hbm = pl.BlockSpec(memory_space=pl.ANY)
    dma = pltpu.SemaphoreType.DMA
    return pl.pallas_call(
        layer_kernel,
        name="layer",
        out_shape=jax.ShapeDtypeStruct((BLOCKS, BLOCK, C), BF16),
        in_specs=[smem, smem, smem, hbm, vmem, vmem, vmem, vmem, vmem, vmem, vmem],
        out_specs=hbm,
        scratch_shapes=[
            pltpu.VMEM((BLOCKS, BLOCK, C), BF16),
            pltpu.VMEM((BLOCKS, BLOCK, C), BF16),
            pltpu.VMEM((BLOCKS, BLOCK, C), BF16),
            pltpu.VMEM((2, STEP_BLOCKS, BLOCK, C), BF16),
            pltpu.VMEM((HEADS, ACC_ROWS, S), F32),
            pltpu.VMEM((PEERS, MSG_ROWS, 128), F32),
            pltpu.VMEM((PEERS, MSG_ROWS, 128), F32),
            pltpu.VMEM((16, 128), F32),
            pltpu.VMEM((PEERS, 16, 128), F32),
            pltpu.VMEM((HEADS, S, 128), BF16),
            dma,
            dma((2, STEP_BLOCKS)),
            dma((PEERS,)),
            dma((PEERS,)),
            dma((PEERS,)),
            dma((PEERS,)),
            dma((PEERS,)),
            dma((PEERS,)),
        ],
        compiler_params=pltpu.CompilerParams(
            collective_id=1, has_side_effects=True, vmem_limit_bytes=VMEM_LIMIT
        ),
    )(source, tally, scale, table, order, flags, feature, middle, score, qkv, final)


def per_device(table, tally, destination, order, softness, entry, score, qkv, final):
    slots = jnp.arange(BLOCKS, dtype=jnp.int32)
    hit = (destination[None, :] == slots[:, None]) & (slots[None, :] < tally[0])
    source = jnp.sum(jnp.where(hit, slots[None, :], 0), axis=1)
    flags = jnp.broadcast_to(
        jnp.sum(hit.astype(F32), axis=1)[:, None, None], (PEERS, 8, 128)
    )
    scale = LOG2E / softness
    empty = jnp.zeros((HEADS // 2, HD, S), BF16)
    score = jnp.stack(
        [
            jnp.concatenate([score[0::2], empty], axis=1),
            jnp.concatenate([empty, score[1::2]], axis=1),
        ],
        axis=1,
    ).reshape(HEADS, 2 * HD, S)
    feature = jnp.transpose(entry[:, :C])
    middle = entry[:, C:]
    qkv = jnp.transpose(qkv).astype(F32)

    return layer(
        source,
        tally,
        scale,
        table.reshape(BLOCKS, BLOCK, C),
        order.reshape(BLOCKS, 1, BLOCK),
        flags,
        feature,
        middle,
        score,
        qkv,
        final,
    ).reshape(BLOCKS * BLOCK, C)


def solution(mesh):
    split = P(("grp", "pts"))
    rows = P(("grp", "pts"), None)
    return jax.shard_map(
        per_device,
        mesh=mesh,
        in_specs=(rows, split, split, rows, P(), P(), P(), P(), P()),
        out_specs=rows,
        check_vma=False,
    )
```

```python
import jax
import jax.numpy as jnp
from jax import lax
from jax.experimental import pallas as pl
from jax.experimental.pallas import tpu as pltpu
from jax.sharding import PartitionSpec as P

F32 = jnp.float32
BF16 = jnp.bfloat16
MESH = pl.DeviceIdType.MESH
LOG2E = 1.4426950408889634
NORM_EPS = 1e-05
SLICE_EPS = 1e-05
HIGHEST = lax.Precision.HIGHEST
NT = (((1,), (1,)), ((), ()))

C = 512
HEADS = 8
S = 256
HD = 64
BLOCK = 128
BLOCKS = 64
PEERS = 64
SIDE = 4
STEP_ROWS = 1024
STEP_BLOCKS = STEP_ROWS // BLOCK
STEPS = BLOCKS * BLOCK // STEP_ROWS
ACC_ROWS = HD + 16
MSG_ROWS = 24
VMEM_LIMIT = 60 << 20
SEND_STEP = 4
SEND_REDUCE = 4
SEND_BATCH = 9
EARLY = 2
PREPARED = 4


def whole(shape):
    return pl.BlockSpec(shape, lambda *_: (0,) * len(shape))


def normalize_rows(rows):
    values = rows.astype(F32)
    centred = values - jnp.mean(values, axis=-1, keepdims=True)
    spread = jnp.mean(centred * centred, axis=-1, keepdims=True)
    return (centred * lax.rsqrt(spread + NORM_EPS)).astype(BF16)


def head_weights(middle, score_ref, scale_ref, head):
    pair = middle[:, (head // 2) * 128 : (head // 2) * 128 + 128]
    scores = jnp.dot(pair, score_ref[head], preferred_element_type=F32)
    powered = jnp.exp2(scores * scale_ref[head])
    return (powered * (1.0 / jnp.sum(powered, axis=-1, keepdims=True))).astype(BF16)


def mix_tokens(tokens_ref, qkv_ref, mixed_ref):
    for head in range(HEADS):
        tokens = jnp.concatenate(
            [
                jnp.concatenate(
                    [tokens_ref[head * 8 + j, 0:8, :], tokens_ref[head * 8 + j, 8:16, :]], axis=1
                )
                for j in range(8)
            ],
            axis=0,
        )
        project = jnp.dot(qkv_ref[...], tokens, preferred_element_type=F32, precision=HIGHEST)
        queries = jnp.transpose(project[0:HD])
        scores = jnp.dot(
            queries, project[HD : 2 * HD], preferred_element_type=F32, precision=HIGHEST
        ) * (HD**-0.5)
        powered = jnp.exp(scores)
        attend = powered / jnp.sum(powered, axis=-1, keepdims=True)
        mixed = lax.dot_general(
            attend, project[2 * HD :], NT, preferred_element_type=F32, precision=HIGHEST
        )
        zeros = jnp.zeros_like(mixed)
        padded = [mixed, zeros] if head % 2 == 0 else [zeros, mixed]
        mixed_ref[head] = jnp.concatenate(padded, axis=1).astype(BF16)


def peer_at(me, i, sign):
    z, x, y = me // 16, (me // 4) % 4, me % 4
    a, b, c = i % 4, (i // 4) % 4, i // 16
    return (
        ((z + sign * a + 8) % SIDE) * 16
        + ((x + sign * (a + b) + 8) % SIDE) * 4
        + (y + sign * (a + c) + 8) % SIDE
    )


def layer_kernel(
    source_ref,
    tally_ref,
    softness_ref,
    destination_ref,
    table_hbm,
    order_ref,
    entry_ref,
    score_in_ref,
    qkv_in_ref,
    final_ref,
    out_hbm,
    table_ref,
    outgoing_ref,
    arrived_ref,
    done_ref,
    weights_ref,
    feature_ref,
    score_ref,
    qkv_ref,
    scale_ref,
    flag_ref,
    acc_ref,
    msg_ref,
    got_ref,
    mine_ref,
    tokens_ref,
    mixed_ref,
    load_sem,
    store_sem,
    block_send,
    block_recv,
    sum_send,
    sum_recv,
    token_send,
    token_recv,
):
    me = lax.axis_index("pts")
    barrier = pltpu.get_barrier_semaphore()
    load = pltpu.make_async_copy(table_hbm, table_ref, load_sem)
    load.start()

    @pl.loop(1, PEERS)
    def _(i):
        pl.semaphore_signal(
            barrier, inc=1, device_id={"pts": peer_at(me, i, 1)}, device_id_type=MESH
        )

    def copy(src, dst, send, recv, i):
        return pltpu.make_async_remote_copy(
            src_ref=src,
            dst_ref=dst,
            send_sem=send.at[i],
            recv_sem=recv.at[i],
            device_id={"pts": peer_at(me, i, 1)},
            device_id_type=MESH,
        )

    def block_copy(i):
        return copy(outgoing_ref.at[i], arrived_ref.at[i], block_send, block_recv, i)

    def sum_copy(i):
        return copy(msg_ref.at[peer_at(me, i, 1)], got_ref.at[i], sum_send, sum_recv, i)

    def token_copy(i):
        return copy(mine_ref, tokens_ref.at[me], token_send, token_recv, i)

    def token_arrival(i):
        return copy(mine_ref, tokens_ref.at[peer_at(me, i, -1)], token_send, token_recv, i)

    columns = lax.broadcasted_iota(jnp.int32, (BLOCK, BLOCK), 1).astype(F32)

    def placed(i):
        b = source_ref[peer_at(me, i, 1)]
        wanted = jnp.broadcast_to(order_ref[b].astype(F32), (BLOCK, BLOCK))
        picking = (jnp.transpose(wanted) == columns).astype(F32).astype(BF16)
        return jnp.dot(picking, table_ref[b], preferred_element_type=F32).astype(BF16)

    def place(first, count):
        for j in range(count):
            outgoing_ref[first + j] = placed(first + j)

    def send(first, count):
        @pl.loop(first, first + count)
        def _(i):
            block_copy(i).start()

    feature_ref[...] = jnp.transpose(entry_ref[:, 0:C])
    qkv_ref[...] = jnp.transpose(qkv_in_ref[...].astype(F32))
    for head in range(HEADS):
        own, other = (head % 2) * HD, (1 - head % 2) * HD
        score_ref[head, own : own + HD, :] = score_in_ref[head]
        score_ref[head, other : other + HD, :] = jnp.zeros((HD, S), BF16)
        scale_ref[head] = LOG2E / jnp.full((1, S), softness_ref[head], F32)
    slot = lax.broadcasted_iota(jnp.int32, (PEERS, BLOCKS), 1)
    peer = lax.broadcasted_iota(jnp.int32, (PEERS, BLOCKS), 0)
    hit = (destination_ref[...] == peer) & (slot < tally_ref[0])
    flag_ref[...] = jnp.broadcast_to(
        jnp.sum(hit.astype(F32), axis=1, keepdims=True), (PEERS, 128)
    )
    acc_ref[...] = jnp.zeros_like(acc_ref)
    load.wait()
    place(1, SEND_STEP)
    pl.semaphore_wait(barrier, PEERS - 1)

    @pl.loop(0, STEPS)
    def _(step):
        first = 1 + step * SEND_STEP
        send(first, SEND_STEP)
        place(first + SEND_STEP, SEND_STEP)
        part = table_ref[pl.ds(step * STEP_BLOCKS, STEP_BLOCKS)].reshape(STEP_ROWS, C)
        normed = normalize_rows(part)
        live = (
            lax.broadcasted_iota(jnp.int32, (1, STEP_ROWS), 1)
            < (tally_ref[0] - step * STEP_BLOCKS) * BLOCK
        ).astype(F32)
        features = lax.dot_general(feature_ref[...], normed, NT, preferred_element_type=F32)
        features = (features * live).astype(BF16)
        ones = jnp.broadcast_to(live, (16, STEP_ROWS)).astype(BF16)
        middle = jnp.dot(normed, entry_ref[:, C:], preferred_element_type=F32).astype(BF16)
        for head in range(HEADS):
            weights = head_weights(middle, score_ref, scale_ref, head)
            left = jnp.concatenate([features[head * HD : head * HD + HD], ones], axis=0)
            acc_ref[head] += jnp.dot(left, weights, preferred_element_type=F32)

    for p in range(PEERS):
        head, part = p // 8, (p % 8) * 8
        msg_ref[p, 0:8, :] = acc_ref[head, part : part + 8, 0:128]
        msg_ref[p, 8:16, :] = acc_ref[head, part : part + 8, 128:256]
        msg_ref[p, 16:17, :] = acc_ref[head, HD : HD + 1, 0:128]
        msg_ref[p, 17:18, :] = acc_ref[head, HD : HD + 1, 128:256]
        msg_ref[p, 18:19, :] = flag_ref[p : p + 1, :]
        msg_ref[p, 19:24, :] = jnp.zeros((5, 128), F32)

    sent = 1 + STEPS * SEND_STEP
    ready = sent + SEND_STEP
    arrived_ref[0] = placed(0)

    @pl.loop(1, PEERS)
    def _(i):
        sum_copy(i).start()

    send(sent, SEND_REDUCE)
    sent += SEND_REDUCE
    place(ready, SEND_BATCH)
    ready += SEND_BATCH

    def wait_group(step):
        for j in range(STEP_BLOCKS):
            i = step * STEP_BLOCKS + j

            @pl.when(i > 0)
            def _():
                block_copy(i).wait_recv()

    def rows_of(step):
        return arrived_ref[pl.ds(step * STEP_BLOCKS, STEP_BLOCKS)].reshape(STEP_ROWS, C)

    def middle_of(step):
        return jnp.dot(
            normalize_rows(rows_of(step)), entry_ref[:, C:], preferred_element_type=F32
        ).astype(BF16)

    def prepare(first, last):
        @pl.loop(first, last)
        def _(step):
            wait_group(step)
            middle = middle_of(step)
            for head in range(HEADS):
                weights_ref[step, head] = head_weights(middle, score_ref, scale_ref, head)

    prepare(0, EARLY)
    got_ref[0] = msg_ref[me]

    def add(i, total):
        sum_copy(i).wait_recv()
        return total + got_ref[i]

    total = lax.fori_loop(1, PEERS, add, got_ref[0])
    mine_ref[0:8, :] = total[0:8] / (total[16:17] + SLICE_EPS)
    mine_ref[8:16, :] = total[8:16] / (total[17:18] + SLICE_EPS)
    tokens_ref[me] = mine_ref[...]

    @pl.loop(1, PEERS)
    def _(i):
        token_copy(i).start()

    while ready < PEERS:
        send(sent, ready - sent)
        sent = ready
        count = min(SEND_BATCH, PEERS - ready)
        place(ready, count)
        ready += count
    send(sent, PEERS - sent)
    prepare(EARLY, PREPARED)

    @pl.loop(1, PEERS)
    def _(i):
        token_arrival(i).wait_recv()

    mix_tokens(tokens_ref, qkv_ref, mixed_ref)

    def store(step, j):
        slot = step % 2
        return pltpu.make_async_copy(
            done_ref.at[slot, j],
            out_hbm.at[peer_at(me, step * STEP_BLOCKS + j, -1)],
            store_sem.at[slot, j],
        )

    def finish(step, weights_of):
        @pl.when(step >= 2)
        def _():
            for j in range(STEP_BLOCKS):
                store(step - 2, j).wait()

        block_rows = rows_of(step)
        spread = []
        for pair in range(HEADS // 2):
            first, second = weights_of(2 * pair), weights_of(2 * pair + 1)
            spread.append(
                (
                    jnp.dot(first, mixed_ref[2 * pair], preferred_element_type=F32)
                    + jnp.dot(second, mixed_ref[2 * pair + 1], preferred_element_type=F32)
                ).astype(BF16)
            )
        spread = jnp.concatenate(spread, axis=1)
        update = jnp.dot(spread, final_ref[...], preferred_element_type=F32)
        for j in range(STEP_BLOCKS):
            flag = got_ref[step * STEP_BLOCKS + j, 18:19, :]
            flag = jnp.concatenate([flag] * (C // 128), axis=1)
            part = slice(j * BLOCK, (j + 1) * BLOCK)
            done_ref[step % 2, j] = (
                (block_rows[part].astype(F32) + update[part]) * flag
            ).astype(BF16)
        for j in range(STEP_BLOCKS):
            store(step, j).start()

    @pl.loop(0, PREPARED)
    def _(step):
        finish(step, lambda head: weights_ref[step, head])

    @pl.loop(PREPARED, STEPS)
    def _(step):
        wait_group(step)
        middle = middle_of(step)
        finish(step, lambda head: head_weights(middle, score_ref, scale_ref, head))

    for step in (STEPS - 2, STEPS - 1):
        for j in range(STEP_BLOCKS):
            store(step, j).wait()

    @pl.loop(1, PEERS)
    def _(i):
        block_copy(i).wait_send()
        sum_copy(i).wait_send()
        token_copy(i).wait_send()


def layer(source, tally, softness, destination, table, order, entry, score, qkv, final):
    smem = pl.BlockSpec(memory_space=pltpu.SMEM)
    vmem = pl.BlockSpec(memory_space=pltpu.VMEM)
    hbm = pl.BlockSpec(memory_space=pl.ANY)
    dma = pltpu.SemaphoreType.DMA
    return pl.pallas_call(
        layer_kernel,
        name="layer",
        out_shape=jax.ShapeDtypeStruct((BLOCKS, BLOCK, C), BF16),
        in_specs=[smem, smem, smem, vmem, hbm, vmem, vmem, vmem, vmem, vmem],
        out_specs=hbm,
        scratch_shapes=[
            pltpu.VMEM((BLOCKS, BLOCK, C), BF16),
            pltpu.VMEM((BLOCKS, BLOCK, C), BF16),
            pltpu.VMEM((BLOCKS, BLOCK, C), BF16),
            pltpu.VMEM((2, STEP_BLOCKS, BLOCK, C), BF16),
            pltpu.VMEM((PREPARED, HEADS, STEP_ROWS, S), BF16),
            pltpu.VMEM((C, C), BF16),
            pltpu.VMEM((HEADS, 2 * HD, S), BF16),
            pltpu.VMEM((3 * HD, HD), F32),
            pltpu.VMEM((HEADS, 1, S), F32),
            pltpu.VMEM((PEERS, 128), F32),
            pltpu.VMEM((HEADS, ACC_ROWS, S), F32),
            pltpu.VMEM((PEERS, MSG_ROWS, 128), F32),
            pltpu.VMEM((PEERS, MSG_ROWS, 128), F32),
            pltpu.VMEM((16, 128), F32),
            pltpu.VMEM((PEERS, 16, 128), F32),
            pltpu.VMEM((HEADS, S, 128), BF16),
            dma,
            dma((2, STEP_BLOCKS)),
            dma((PEERS,)),
            dma((PEERS,)),
            dma((PEERS,)),
            dma((PEERS,)),
            dma((PEERS,)),
            dma((PEERS,)),
        ],
        compiler_params=pltpu.CompilerParams(
            collective_id=1, has_side_effects=True, vmem_limit_bytes=VMEM_LIMIT
        ),
    )(source, tally, softness, destination, table, order, entry, score, qkv, final)


def per_device(table, tally, destination, order, softness, entry, score, qkv, final):
    slots = jnp.arange(BLOCKS, dtype=jnp.int32)
    hit = (destination[None, :] == slots[:, None]) & (slots[None, :] < tally[0])
    source = jnp.sum(jnp.where(hit, slots[None, :], 0), axis=1)
    return layer(
        source,
        tally,
        softness,
        destination.reshape(1, BLOCKS),
        table.reshape(BLOCKS, BLOCK, C),
        order.reshape(BLOCKS, 1, BLOCK),
        entry,
        score,
        qkv,
        final,
    ).reshape(BLOCKS * BLOCK, C)


def solution(mesh):
    split = P(("grp", "pts"))
    rows = P(("grp", "pts"), None)
    return jax.shard_map(
        per_device,
        mesh=mesh,
        in_specs=(rows, split, split, rows, P(), P(), P(), P(), P()),
        out_specs=rows,
        check_vma=False,
    )
```

```python
import jax
import jax.numpy as jnp
from jax import lax
from jax.experimental import pallas as pl
from jax.experimental.pallas import tpu as pltpu
from jax.sharding import PartitionSpec as P

F32 = jnp.float32
BF16 = jnp.bfloat16
MESH = pl.DeviceIdType.MESH
LOG2E = 1.4426950408889634
NORM_EPS = 1e-05
SLICE_EPS = 1e-05
HIGHEST = lax.Precision.HIGHEST
NT = (((1,), (1,)), ((), ()))

C = 512
HEADS = 8
S = 256
HD = 64
BLOCK = 128
BLOCKS = 64
PEERS = 64
SIDE = 4
STEP_ROWS = 1024
STEP_BLOCKS = STEP_ROWS // BLOCK
STEPS = BLOCKS * BLOCK // STEP_ROWS
ACC_ROWS = HD + 16
MSG_ROWS = 24
VMEM_LIMIT = 60 << 20
SEND_STEP = 8
SEND_STEPS = 4
SEND_REDUCE = 0
SEND_BATCH = 9
EARLY = 2
PREPARED = 4


def whole(shape):
    return pl.BlockSpec(shape, lambda *_: (0,) * len(shape))


def normalize_rows(rows):
    values = rows.astype(F32)
    centred = values - jnp.mean(values, axis=-1, keepdims=True)
    spread = jnp.mean(centred * centred, axis=-1, keepdims=True)
    return (centred * lax.rsqrt(spread + NORM_EPS)).astype(BF16)


def head_weights(middle, score_ref, scale_ref, head):
    pair = middle[:, (head // 2) * 128 : (head // 2) * 128 + 128]
    scores = jnp.dot(pair, score_ref[head], preferred_element_type=F32)
    powered = jnp.exp2(scores * scale_ref[head])
    return (powered * (1.0 / jnp.sum(powered, axis=-1, keepdims=True))).astype(BF16)


def mix_tokens(tokens_ref, qkv_ref, mixed_ref):
    for head in range(HEADS):
        tokens = jnp.concatenate(
            [
                jnp.concatenate(
                    [tokens_ref[head * 8 + j, 0:8, :], tokens_ref[head * 8 + j, 8:16, :]], axis=1
                )
                for j in range(8)
            ],
            axis=0,
        )
        project = jnp.dot(qkv_ref[...], tokens, preferred_element_type=F32, precision=HIGHEST)
        queries = jnp.transpose(project[0:HD])
        scores = jnp.dot(
            queries, project[HD : 2 * HD], preferred_element_type=F32, precision=HIGHEST
        ) * (HD**-0.5)
        powered = jnp.exp(scores)
        attend = powered / jnp.sum(powered, axis=-1, keepdims=True)
        mixed = lax.dot_general(
            attend, project[2 * HD :], NT, preferred_element_type=F32, precision=HIGHEST
        )
        zeros = jnp.zeros_like(mixed)
        padded = [mixed, zeros] if head % 2 == 0 else [zeros, mixed]
        mixed_ref[head] = jnp.concatenate(padded, axis=1).astype(BF16)


def peer_at(me, i, sign):
    z, x, y = me // 16, (me // 4) % 4, me % 4
    a, b, c = i % 4, (i // 4) % 4, i // 16
    return (
        ((z + sign * a + 8) % SIDE) * 16
        + ((x + sign * (a + b) + 8) % SIDE) * 4
        + (y + sign * (a + c) + 8) % SIDE
    )


def layer_kernel(
    source_ref,
    tally_ref,
    softness_ref,
    destination_ref,
    table_hbm,
    order_ref,
    entry_ref,
    score_in_ref,
    qkv_in_ref,
    final_ref,
    out_hbm,
    table_ref,
    outgoing_ref,
    arrived_ref,
    done_ref,
    weights_ref,
    feature_ref,
    score_ref,
    qkv_ref,
    scale_ref,
    flag_ref,
    acc_ref,
    msg_ref,
    got_ref,
    mine_ref,
    tokens_ref,
    mixed_ref,
    load_sem,
    store_sem,
    block_send,
    block_recv,
    sum_send,
    sum_recv,
    token_send,
    token_recv,
):
    me = lax.axis_index("pts")
    barrier = pltpu.get_barrier_semaphore()
    load = pltpu.make_async_copy(table_hbm, table_ref, load_sem)
    load.start()

    @pl.loop(1, PEERS)
    def _(i):
        pl.semaphore_signal(
            barrier, inc=1, device_id={"pts": peer_at(me, i, 1)}, device_id_type=MESH
        )

    def copy(src, dst, send, recv, i):
        return pltpu.make_async_remote_copy(
            src_ref=src,
            dst_ref=dst,
            send_sem=send.at[i],
            recv_sem=recv.at[i],
            device_id={"pts": peer_at(me, i, 1)},
            device_id_type=MESH,
        )

    def block_copy(i):
        return copy(outgoing_ref.at[i], arrived_ref.at[i], block_send, block_recv, i)

    def sum_copy(i):
        return copy(msg_ref.at[peer_at(me, i, 1)], got_ref.at[i], sum_send, sum_recv, i)

    def token_copy(i):
        return copy(mine_ref, tokens_ref.at[me], token_send, token_recv, i)

    def token_arrival(i):
        return copy(mine_ref, tokens_ref.at[peer_at(me, i, -1)], token_send, token_recv, i)

    columns = lax.broadcasted_iota(jnp.int32, (BLOCK, BLOCK), 1).astype(F32)

    def placed(i):
        b = source_ref[peer_at(me, i, 1)]
        wanted = jnp.broadcast_to(order_ref[b].astype(F32), (BLOCK, BLOCK))
        picking = (jnp.transpose(wanted) == columns).astype(F32).astype(BF16)
        return jnp.dot(picking, table_ref[b], preferred_element_type=F32).astype(BF16)

    def place(first, count):
        for j in range(count):
            outgoing_ref[first + j] = placed(first + j)

    def send(first, count):
        @pl.loop(first, first + count)
        def _(i):
            block_copy(i).start()

    feature_ref[...] = jnp.transpose(entry_ref[:, 0:C])
    qkv_ref[...] = jnp.transpose(qkv_in_ref[...].astype(F32))
    for head in range(HEADS):
        own, other = (head % 2) * HD, (1 - head % 2) * HD
        score_ref[head, own : own + HD, :] = score_in_ref[head]
        score_ref[head, other : other + HD, :] = jnp.zeros((HD, S), BF16)
        scale_ref[head] = LOG2E / jnp.full((1, S), softness_ref[head], F32)
    slot = lax.broadcasted_iota(jnp.int32, (PEERS, BLOCKS), 1)
    peer = lax.broadcasted_iota(jnp.int32, (PEERS, BLOCKS), 0)
    hit = (destination_ref[...] == peer) & (slot < tally_ref[0])
    flag_ref[...] = jnp.broadcast_to(
        jnp.sum(hit.astype(F32), axis=1, keepdims=True), (PEERS, 128)
    )
    acc_ref[...] = jnp.zeros_like(acc_ref)
    load.wait()
    place(1, SEND_STEP)
    pl.semaphore_wait(barrier, PEERS - 1)

    @pl.loop(0, STEPS)
    def _(step):
        @pl.when(step < SEND_STEPS)
        def _():
            first = 1 + step * SEND_STEP
            send(first, SEND_STEP)
            place(first + SEND_STEP, SEND_STEP)

        part = table_ref[pl.ds(step * STEP_BLOCKS, STEP_BLOCKS)].reshape(STEP_ROWS, C)
        normed = normalize_rows(part)
        live = (
            lax.broadcasted_iota(jnp.int32, (1, STEP_ROWS), 1)
            < (tally_ref[0] - step * STEP_BLOCKS) * BLOCK
        ).astype(F32)
        features = lax.dot_general(feature_ref[...], normed, NT, preferred_element_type=F32)
        features = (features * live).astype(BF16)
        ones = jnp.broadcast_to(live, (16, STEP_ROWS)).astype(BF16)
        middle = jnp.dot(normed, entry_ref[:, C:], preferred_element_type=F32).astype(BF16)
        for head in range(HEADS):
            weights = head_weights(middle, score_ref, scale_ref, head)
            left = jnp.concatenate([features[head * HD : head * HD + HD], ones], axis=0)
            acc_ref[head] += jnp.dot(left, weights, preferred_element_type=F32)

    for p in range(PEERS):
        head, part = p // 8, (p % 8) * 8
        msg_ref[p, 0:8, :] = acc_ref[head, part : part + 8, 0:128]
        msg_ref[p, 8:16, :] = acc_ref[head, part : part + 8, 128:256]
        msg_ref[p, 16:17, :] = acc_ref[head, HD : HD + 1, 0:128]
        msg_ref[p, 17:18, :] = acc_ref[head, HD : HD + 1, 128:256]
        msg_ref[p, 18:19, :] = flag_ref[p : p + 1, :]
        msg_ref[p, 19:24, :] = jnp.zeros((5, 128), F32)

    sent = 1 + SEND_STEPS * SEND_STEP
    ready = sent + SEND_STEP
    arrived_ref[0] = placed(0)

    @pl.loop(1, PEERS)
    def _(i):
        sum_copy(i).start()

    if SEND_REDUCE:
        send(sent, SEND_REDUCE)
        sent += SEND_REDUCE
    place(ready, SEND_BATCH)
    ready += SEND_BATCH

    def wait_group(step):
        for j in range(STEP_BLOCKS):
            i = step * STEP_BLOCKS + j

            @pl.when(i > 0)
            def _():
                block_copy(i).wait_recv()

    def rows_of(step):
        return arrived_ref[pl.ds(step * STEP_BLOCKS, STEP_BLOCKS)].reshape(STEP_ROWS, C)

    def middle_of(step):
        return jnp.dot(
            normalize_rows(rows_of(step)), entry_ref[:, C:], preferred_element_type=F32
        ).astype(BF16)

    def prepare(first, last):
        @pl.loop(first, last)
        def _(step):
            wait_group(step)
            middle = middle_of(step)
            for head in range(HEADS):
                weights_ref[step, head] = head_weights(middle, score_ref, scale_ref, head)

    prepare(0, EARLY)
    got_ref[0] = msg_ref[me]

    def add(i, total):
        sum_copy(i).wait_recv()
        return total + got_ref[i]

    total = lax.fori_loop(1, PEERS, add, got_ref[0])
    mine_ref[0:8, :] = total[0:8] / (total[16:17] + SLICE_EPS)
    mine_ref[8:16, :] = total[8:16] / (total[17:18] + SLICE_EPS)
    tokens_ref[me] = mine_ref[...]

    @pl.loop(1, PEERS)
    def _(i):
        token_copy(i).start()

    while ready < PEERS:
        send(sent, ready - sent)
        sent = ready
        count = min(SEND_BATCH, PEERS - ready)
        place(ready, count)
        ready += count
    send(sent, PEERS - sent)
    prepare(EARLY, PREPARED)

    @pl.loop(1, PEERS)
    def _(i):
        token_arrival(i).wait_recv()

    mix_tokens(tokens_ref, qkv_ref, mixed_ref)

    def store(step, j):
        slot = step % 2
        return pltpu.make_async_copy(
            done_ref.at[slot, j],
            out_hbm.at[peer_at(me, step * STEP_BLOCKS + j, -1)],
            store_sem.at[slot, j],
        )

    def finish(step, weights_of):
        @pl.when(step >= 2)
        def _():
            for j in range(STEP_BLOCKS):
                store(step - 2, j).wait()

        block_rows = rows_of(step)
        spread = []
        for pair in range(HEADS // 2):
            first, second = weights_of(2 * pair), weights_of(2 * pair + 1)
            spread.append(
                (
                    jnp.dot(first, mixed_ref[2 * pair], preferred_element_type=F32)
                    + jnp.dot(second, mixed_ref[2 * pair + 1], preferred_element_type=F32)
                ).astype(BF16)
            )
        spread = jnp.concatenate(spread, axis=1)
        update = jnp.dot(spread, final_ref[...], preferred_element_type=F32)
        for j in range(STEP_BLOCKS):
            flag = got_ref[step * STEP_BLOCKS + j, 18:19, :]
            flag = jnp.concatenate([flag] * (C // 128), axis=1)
            part = slice(j * BLOCK, (j + 1) * BLOCK)
            done_ref[step % 2, j] = (
                (block_rows[part].astype(F32) + update[part]) * flag
            ).astype(BF16)
        for j in range(STEP_BLOCKS):
            store(step, j).start()

    @pl.loop(0, PREPARED)
    def _(step):
        finish(step, lambda head: weights_ref[step, head])

    @pl.loop(PREPARED, STEPS)
    def _(step):
        wait_group(step)
        middle = middle_of(step)
        finish(step, lambda head: head_weights(middle, score_ref, scale_ref, head))

    for step in (STEPS - 2, STEPS - 1):
        for j in range(STEP_BLOCKS):
            store(step, j).wait()

    @pl.loop(1, PEERS)
    def _(i):
        block_copy(i).wait_send()
        sum_copy(i).wait_send()
        token_copy(i).wait_send()


def layer(source, tally, softness, destination, table, order, entry, score, qkv, final):
    smem = pl.BlockSpec(memory_space=pltpu.SMEM)
    vmem = pl.BlockSpec(memory_space=pltpu.VMEM)
    hbm = pl.BlockSpec(memory_space=pl.ANY)
    dma = pltpu.SemaphoreType.DMA
    return pl.pallas_call(
        layer_kernel,
        name="layer",
        out_shape=jax.ShapeDtypeStruct((BLOCKS, BLOCK, C), BF16),
        in_specs=[smem, smem, smem, vmem, hbm, vmem, vmem, vmem, vmem, vmem],
        out_specs=hbm,
        scratch_shapes=[
            pltpu.VMEM((BLOCKS, BLOCK, C), BF16),
            pltpu.VMEM((BLOCKS, BLOCK, C), BF16),
            pltpu.VMEM((BLOCKS, BLOCK, C), BF16),
            pltpu.VMEM((2, STEP_BLOCKS, BLOCK, C), BF16),
            pltpu.VMEM((PREPARED, HEADS, STEP_ROWS, S), BF16),
            pltpu.VMEM((C, C), BF16),
            pltpu.VMEM((HEADS, 2 * HD, S), BF16),
            pltpu.VMEM((3 * HD, HD), F32),
            pltpu.VMEM((HEADS, 1, S), F32),
            pltpu.VMEM((PEERS, 128), F32),
            pltpu.VMEM((HEADS, ACC_ROWS, S), F32),
            pltpu.VMEM((PEERS, MSG_ROWS, 128), F32),
            pltpu.VMEM((PEERS, MSG_ROWS, 128), F32),
            pltpu.VMEM((16, 128), F32),
            pltpu.VMEM((PEERS, 16, 128), F32),
            pltpu.VMEM((HEADS, S, 128), BF16),
            dma,
            dma((2, STEP_BLOCKS)),
            dma((PEERS,)),
            dma((PEERS,)),
            dma((PEERS,)),
            dma((PEERS,)),
            dma((PEERS,)),
            dma((PEERS,)),
        ],
        compiler_params=pltpu.CompilerParams(
            collective_id=1, has_side_effects=True, vmem_limit_bytes=VMEM_LIMIT
        ),
    )(source, tally, softness, destination, table, order, entry, score, qkv, final)


def per_device(table, tally, destination, order, softness, entry, score, qkv, final):
    slots = jnp.arange(BLOCKS, dtype=jnp.int32)
    hit = (destination[None, :] == slots[:, None]) & (slots[None, :] < tally[0])
    source = jnp.sum(jnp.where(hit, slots[None, :], 0), axis=1)
    return layer(
        source,
        tally,
        softness,
        destination.reshape(1, BLOCKS),
        table.reshape(BLOCKS, BLOCK, C),
        order.reshape(BLOCKS, 1, BLOCK),
        entry,
        score,
        qkv,
        final,
    ).reshape(BLOCKS * BLOCK, C)


def solution(mesh):
    split = P(("grp", "pts"))
    rows = P(("grp", "pts"), None)
    return jax.shard_map(
        per_device,
        mesh=mesh,
        in_specs=(rows, split, split, rows, P(), P(), P(), P(), P()),
        out_specs=rows,
        check_vma=False,
    )
```

```python
import jax
import jax.numpy as jnp
from jax import lax
from jax.experimental import pallas as pl
from jax.experimental.pallas import tpu as pltpu
from jax.sharding import PartitionSpec as P

F32 = jnp.float32
BF16 = jnp.bfloat16
MESH = pl.DeviceIdType.MESH
LOG2E = 1.4426950408889634
NORM_EPS = 1e-05
SLICE_EPS = 1e-05
HIGHEST = lax.Precision.HIGHEST
NT = (((1,), (1,)), ((), ()))

C = 512
HEADS = 8
S = 256
HD = 64
BLOCK = 128
BLOCKS = 64
PEERS = 64
SIDE = 4
STEP_ROWS = 1024
STEP_BLOCKS = STEP_ROWS // BLOCK
STEPS = BLOCKS * BLOCK // STEP_ROWS
ACC_ROWS = HD + 16
MSG_ROWS = 24
VMEM_LIMIT = 60 << 20
SEND_STEP = 8
SEND_STEPS = 4
SEND_REDUCE = 0
SEND_BATCH = 9
EARLY = 2
PREPARED = 4


def whole(shape):
    return pl.BlockSpec(shape, lambda *_: (0,) * len(shape))


def normalize_rows(rows):
    values = rows.astype(F32)
    centred = values - jnp.mean(values, axis=-1, keepdims=True)
    spread = jnp.mean(centred * centred, axis=-1, keepdims=True)
    return (centred * lax.rsqrt(spread + NORM_EPS)).astype(BF16)


def head_weights(middle, score_ref, scale_ref, head):
    pair = middle[:, (head // 2) * 128 : (head // 2) * 128 + 128]
    scores = jnp.dot(pair, score_ref[head], preferred_element_type=F32)
    powered = jnp.exp2(scores * scale_ref[head])
    return (powered * (1.0 / jnp.sum(powered, axis=-1, keepdims=True))).astype(BF16)


def mix_tokens(tokens_ref, qkv_ref, mixed_ref):
    for head in range(HEADS):
        tokens = jnp.concatenate(
            [
                jnp.concatenate(
                    [tokens_ref[head * 8 + j, 0:8, :], tokens_ref[head * 8 + j, 8:16, :]], axis=1
                )
                for j in range(8)
            ],
            axis=0,
        )
        project = jnp.dot(qkv_ref[...], tokens, preferred_element_type=F32, precision=HIGHEST)
        queries = jnp.transpose(project[0:HD])
        scores = jnp.dot(
            queries, project[HD : 2 * HD], preferred_element_type=F32, precision=HIGHEST
        ) * (HD**-0.5)
        powered = jnp.exp(scores)
        attend = powered / jnp.sum(powered, axis=-1, keepdims=True)
        mixed = lax.dot_general(
            attend, project[2 * HD :], NT, preferred_element_type=F32, precision=HIGHEST
        )
        zeros = jnp.zeros_like(mixed)
        padded = [mixed, zeros] if head % 2 == 0 else [zeros, mixed]
        mixed_ref[head] = jnp.concatenate(padded, axis=1).astype(BF16)


def peer_at(me, i, sign):
    z, x, y = me // 16, (me // 4) % 4, me % 4
    a, b, c = i % 4, (i // 4) % 4, i // 16
    return (
        ((z + sign * a + 8) % SIDE) * 16
        + ((x + sign * (a + b) + 8) % SIDE) * 4
        + (y + sign * (a + c) + 8) % SIDE
    )


def finish_rows(block_rows, weights_of, mixed_ref, final_ref, flag_of, done_ref):
    spread = []
    for pair in range(HEADS // 2):
        first, second = weights_of(2 * pair), weights_of(2 * pair + 1)
        spread.append(
            (
                jnp.dot(first, mixed_ref[2 * pair], preferred_element_type=F32)
                + jnp.dot(second, mixed_ref[2 * pair + 1], preferred_element_type=F32)
            ).astype(BF16)
        )
    spread = jnp.concatenate(spread, axis=1)
    update = jnp.dot(spread, final_ref[...], preferred_element_type=F32)
    for j in range(block_rows.shape[0] // BLOCK):
        flag = flag_of(j)
        flag = jnp.concatenate([flag] * (C // 128), axis=1)
        part = slice(j * BLOCK, (j + 1) * BLOCK)
        done_ref[j] = ((block_rows[part].astype(F32) + update[part]) * flag).astype(BF16)


def prepare_scores(score_in_ref, softness_ref, score_ref, scale_ref):
    for head in range(HEADS):
        own, other = (head % 2) * HD, (1 - head % 2) * HD
        score_ref[head, own : own + HD, :] = score_in_ref[head]
        score_ref[head, other : other + HD, :] = jnp.zeros((HD, S), BF16)
        scale_ref[head] = LOG2E / jnp.full((1, S), softness_ref[head], F32)


def settle_kernel(
    softness_ref,
    blocks_hbm,
    mixed_ref,
    flags_ref,
    entry_ref,
    score_in_ref,
    final_ref,
    out_hbm,
    rows_ref,
    score_ref,
    scale_ref,
    load_sem,
    store_sem,
):
    me = lax.axis_index("pts")

    def load(step):
        part = pl.ds(step * STEP_BLOCKS, STEP_BLOCKS)
        return pltpu.make_async_copy(blocks_hbm.at[part], rows_ref.at[part], load_sem.at[step])

    def store(i):
        return pltpu.make_async_copy(
            rows_ref.at[i], out_hbm.at[peer_at(me, i, -1)], store_sem.at[i]
        )

    load(STEPS - 1).start()
    for step in range(STEPS - 1):
        load(step).start()
    prepare_scores(score_in_ref, softness_ref, score_ref, scale_ref)
    load(STEPS - 1).wait()
    count = STEP_BLOCKS // 2
    for half in range(2):
        first = (STEPS - 1) * STEP_BLOCKS + half * count
        block_rows = rows_ref[first : first + count].reshape(count * BLOCK, C)
        middle = jnp.dot(
            normalize_rows(block_rows), entry_ref[:, C:], preferred_element_type=F32
        ).astype(BF16)
        finish_rows(
            block_rows,
            lambda head: head_weights(middle, score_ref, scale_ref, head),
            mixed_ref,
            final_ref,
            lambda j: flags_ref[first + j, 2:3, :],
            rows_ref.at[pl.ds(first, count)],
        )
        if half == 0:
            for step in range(STEPS - 1):
                load(step).wait()

                @pl.loop(step * STEP_BLOCKS, (step + 1) * STEP_BLOCKS)
                def _(i):
                    store(i).start()

        @pl.loop(first, first + count)
        def _(i):
            store(i).start()

    @pl.loop(0, BLOCKS)
    def _(i):
        store(i).wait()


def settle(softness, blocks, mixed, flags, entry, score, final):
    smem = pl.BlockSpec(memory_space=pltpu.SMEM)
    vmem = pl.BlockSpec(memory_space=pltpu.VMEM)
    hbm = pl.BlockSpec(memory_space=pl.ANY)
    return pl.pallas_call(
        settle_kernel,
        name="settle",
        out_shape=jax.ShapeDtypeStruct((BLOCKS, BLOCK, C), BF16),
        in_specs=[smem, hbm, vmem, vmem, vmem, vmem, vmem],
        out_specs=hbm,
        scratch_shapes=[
            pltpu.VMEM((BLOCKS, BLOCK, C), BF16),
            pltpu.VMEM((HEADS, 2 * HD, S), BF16),
            pltpu.VMEM((HEADS, 1, S), F32),
            pltpu.SemaphoreType.DMA((STEPS,)),
            pltpu.SemaphoreType.DMA((BLOCKS,)),
        ],
        compiler_params=pltpu.CompilerParams(vmem_limit_bytes=VMEM_LIMIT),
    )(softness, blocks, mixed, flags, entry, score, final)


def layer_kernel(
    source_ref,
    tally_ref,
    softness_ref,
    destination_ref,
    table_hbm,
    order_ref,
    entry_ref,
    score_in_ref,
    qkv_in_ref,
    final_ref,
    out_hbm,
    mixed_hbm,
    flags_hbm,
    table_ref,
    outgoing_ref,
    arrived_ref,
    done_ref,
    weights_ref,
    feature_ref,
    score_ref,
    qkv_ref,
    scale_ref,
    flag_ref,
    acc_ref,
    msg_ref,
    got_ref,
    mine_ref,
    tokens_ref,
    mixed_ref,
    load_sem,
    store_sem,
    extra_sem,
    block_send,
    block_recv,
    sum_send,
    sum_recv,
    token_send,
    token_recv,
):
    me = lax.axis_index("pts")
    barrier = pltpu.get_barrier_semaphore()
    load = pltpu.make_async_copy(table_hbm, table_ref, load_sem)
    load.start()

    @pl.loop(1, PEERS)
    def _(i):
        pl.semaphore_signal(
            barrier, inc=1, device_id={"pts": peer_at(me, i, 1)}, device_id_type=MESH
        )

    def copy(src, dst, send, recv, i):
        return pltpu.make_async_remote_copy(
            src_ref=src,
            dst_ref=dst,
            send_sem=send.at[i],
            recv_sem=recv.at[i],
            device_id={"pts": peer_at(me, i, 1)},
            device_id_type=MESH,
        )

    def block_copy(i):
        return copy(outgoing_ref.at[i], arrived_ref.at[i], block_send, block_recv, i)

    def sum_copy(i):
        return copy(msg_ref.at[peer_at(me, i, 1)], got_ref.at[i], sum_send, sum_recv, i)

    def token_copy(i):
        return copy(mine_ref, tokens_ref.at[me], token_send, token_recv, i)

    def token_arrival(i):
        return copy(mine_ref, tokens_ref.at[peer_at(me, i, -1)], token_send, token_recv, i)

    columns = lax.broadcasted_iota(jnp.int32, (BLOCK, BLOCK), 1).astype(F32)

    def placed(i):
        b = source_ref[peer_at(me, i, 1)]
        wanted = jnp.broadcast_to(order_ref[b].astype(F32), (BLOCK, BLOCK))
        picking = (jnp.transpose(wanted) == columns).astype(F32).astype(BF16)
        return jnp.dot(picking, table_ref[b], preferred_element_type=F32).astype(BF16)

    def place(first, count):
        for j in range(count):
            outgoing_ref[first + j] = placed(first + j)

    def send(first, count):
        @pl.loop(first, first + count)
        def _(i):
            block_copy(i).start()

    feature_ref[...] = jnp.transpose(entry_ref[:, 0:C])
    qkv_ref[...] = jnp.transpose(qkv_in_ref[...].astype(F32))
    prepare_scores(score_in_ref, softness_ref, score_ref, scale_ref)
    slot = lax.broadcasted_iota(jnp.int32, (PEERS, BLOCKS), 1)
    peer = lax.broadcasted_iota(jnp.int32, (PEERS, BLOCKS), 0)
    hit = (destination_ref[...] == peer) & (slot < tally_ref[0])
    flag_ref[...] = jnp.broadcast_to(
        jnp.sum(hit.astype(F32), axis=1, keepdims=True), (PEERS, 128)
    )
    acc_ref[...] = jnp.zeros_like(acc_ref)
    load.wait()
    place(1, SEND_STEP)
    pl.semaphore_wait(barrier, PEERS - 1)

    @pl.loop(0, STEPS)
    def _(step):
        @pl.when(step < SEND_STEPS)
        def _():
            first = 1 + step * SEND_STEP
            send(first, SEND_STEP)
            place(first + SEND_STEP, SEND_STEP)

        part = table_ref[pl.ds(step * STEP_BLOCKS, STEP_BLOCKS)].reshape(STEP_ROWS, C)
        normed = normalize_rows(part)
        live = (
            lax.broadcasted_iota(jnp.int32, (1, STEP_ROWS), 1)
            < (tally_ref[0] - step * STEP_BLOCKS) * BLOCK
        ).astype(F32)
        features = lax.dot_general(feature_ref[...], normed, NT, preferred_element_type=F32)
        features = (features * live).astype(BF16)
        ones = jnp.broadcast_to(live, (16, STEP_ROWS)).astype(BF16)
        middle = jnp.dot(normed, entry_ref[:, C:], preferred_element_type=F32).astype(BF16)
        for head in range(HEADS):
            weights = head_weights(middle, score_ref, scale_ref, head)
            left = jnp.concatenate([features[head * HD : head * HD + HD], ones], axis=0)
            acc_ref[head] += jnp.dot(left, weights, preferred_element_type=F32)

    for p in range(PEERS):
        head, part = p // 8, (p % 8) * 8
        msg_ref[p, 0:8, :] = acc_ref[head, part : part + 8, 0:128]
        msg_ref[p, 8:16, :] = acc_ref[head, part : part + 8, 128:256]
        msg_ref[p, 16:17, :] = acc_ref[head, HD : HD + 1, 0:128]
        msg_ref[p, 17:18, :] = acc_ref[head, HD : HD + 1, 128:256]
        msg_ref[p, 18:19, :] = flag_ref[p : p + 1, :]
        msg_ref[p, 19:24, :] = jnp.zeros((5, 128), F32)

    sent = 1 + SEND_STEPS * SEND_STEP
    ready = sent + SEND_STEP
    arrived_ref[0] = placed(0)

    @pl.loop(1, PEERS)
    def _(i):
        sum_copy(i).start()

    if SEND_REDUCE:
        send(sent, SEND_REDUCE)
        sent += SEND_REDUCE
    place(ready, SEND_BATCH)
    ready += SEND_BATCH

    def wait_group(step):
        for j in range(STEP_BLOCKS):
            i = step * STEP_BLOCKS + j

            @pl.when(i > 0)
            def _():
                block_copy(i).wait_recv()

    def rows_of(step):
        return arrived_ref[pl.ds(step * STEP_BLOCKS, STEP_BLOCKS)].reshape(STEP_ROWS, C)

    def middle_of(step):
        return jnp.dot(
            normalize_rows(rows_of(step)), entry_ref[:, C:], preferred_element_type=F32
        ).astype(BF16)

    def prepare(first, last):
        @pl.loop(first, last)
        def _(step):
            wait_group(step)
            middle = middle_of(step)
            for head in range(HEADS):
                weights_ref[step, head] = head_weights(middle, score_ref, scale_ref, head)

    prepare(0, EARLY)
    got_ref[0] = msg_ref[me]

    def add(i, total):
        sum_copy(i).wait_recv()
        return total + got_ref[i]

    total = lax.fori_loop(1, PEERS, add, got_ref[0])
    mine_ref[0:8, :] = total[0:8] / (total[16:17] + SLICE_EPS)
    mine_ref[8:16, :] = total[8:16] / (total[17:18] + SLICE_EPS)
    tokens_ref[me] = mine_ref[...]

    @pl.loop(1, PEERS)
    def _(i):
        token_copy(i).start()

    while ready < PEERS:
        send(sent, ready - sent)
        sent = ready
        count = min(SEND_BATCH, PEERS - ready)
        place(ready, count)
        ready += count
    send(sent, PEERS - sent)
    prepare(EARLY, PREPARED)

    @pl.loop(1, PEERS)
    def _(i):
        token_arrival(i).wait_recv()

    mix_tokens(tokens_ref, qkv_ref, mixed_ref)

    share_mixed = pltpu.make_async_copy(mixed_ref, mixed_hbm, extra_sem.at[0])
    share_flags = pltpu.make_async_copy(
        got_ref.at[:, pl.ds(16, 8), :], flags_hbm, extra_sem.at[1]
    )
    share_flags.start()
    share_mixed.start()

    def store(step):
        return pltpu.make_async_copy(
            done_ref.at[step % 2],
            out_hbm.at[pl.ds(step * STEP_BLOCKS, STEP_BLOCKS)],
            store_sem.at[step % 2],
        )

    def finish(step, weights_of):
        @pl.when(step >= 2)
        def _():
            store(step - 2).wait()

        finish_rows(
            rows_of(step),
            weights_of,
            mixed_ref,
            final_ref,
            lambda j: got_ref[step * STEP_BLOCKS + j, 18:19, :],
            done_ref.at[step % 2],
        )
        store(step).start()

    @pl.loop(0, PREPARED)
    def _(step):
        finish(step, lambda head: weights_ref[step, head])

    @pl.loop(PREPARED, STEPS - 1)
    def _(step):
        wait_group(step)
        middle = middle_of(step)
        finish(step, lambda head: head_weights(middle, score_ref, scale_ref, head))

    wait_group(STEPS - 1)
    last = pl.ds((STEPS - 1) * STEP_BLOCKS, STEP_BLOCKS)
    rest = pltpu.make_async_copy(arrived_ref.at[last], out_hbm.at[last], extra_sem.at[2])
    rest.start()
    store(STEPS - 3).wait()
    store(STEPS - 2).wait()
    share_flags.wait()
    share_mixed.wait()

    @pl.loop(1, PEERS)
    def _(i):
        block_copy(i).wait_send()
        sum_copy(i).wait_send()
        token_copy(i).wait_send()

    rest.wait()


def layer(source, tally, softness, destination, table, order, entry, score, qkv, final):
    smem = pl.BlockSpec(memory_space=pltpu.SMEM)
    vmem = pl.BlockSpec(memory_space=pltpu.VMEM)
    hbm = pl.BlockSpec(memory_space=pl.ANY)
    dma = pltpu.SemaphoreType.DMA
    return pl.pallas_call(
        layer_kernel,
        name="layer",
        out_shape=(
            jax.ShapeDtypeStruct((BLOCKS, BLOCK, C), BF16),
            jax.ShapeDtypeStruct((HEADS, S, 128), BF16),
            jax.ShapeDtypeStruct((PEERS, 8, 128), F32),
        ),
        in_specs=[smem, smem, smem, vmem, hbm, vmem, vmem, vmem, vmem, vmem],
        out_specs=[hbm, hbm, hbm],
        scratch_shapes=[
            pltpu.VMEM((BLOCKS, BLOCK, C), BF16),
            pltpu.VMEM((BLOCKS, BLOCK, C), BF16),
            pltpu.VMEM((BLOCKS, BLOCK, C), BF16),
            pltpu.VMEM((2, STEP_BLOCKS, BLOCK, C), BF16),
            pltpu.VMEM((PREPARED, HEADS, STEP_ROWS, S), BF16),
            pltpu.VMEM((C, C), BF16),
            pltpu.VMEM((HEADS, 2 * HD, S), BF16),
            pltpu.VMEM((3 * HD, HD), F32),
            pltpu.VMEM((HEADS, 1, S), F32),
            pltpu.VMEM((PEERS, 128), F32),
            pltpu.VMEM((HEADS, ACC_ROWS, S), F32),
            pltpu.VMEM((PEERS, MSG_ROWS, 128), F32),
            pltpu.VMEM((PEERS, MSG_ROWS, 128), F32),
            pltpu.VMEM((16, 128), F32),
            pltpu.VMEM((PEERS, 16, 128), F32),
            pltpu.VMEM((HEADS, S, 128), BF16),
            dma,
            dma((2,)),
            dma((3,)),
            dma((PEERS,)),
            dma((PEERS,)),
            dma((PEERS,)),
            dma((PEERS,)),
            dma((PEERS,)),
            dma((PEERS,)),
        ],
        compiler_params=pltpu.CompilerParams(
            collective_id=1, has_side_effects=True, vmem_limit_bytes=VMEM_LIMIT
        ),
    )(source, tally, softness, destination, table, order, entry, score, qkv, final)


def per_device(table, tally, destination, order, softness, entry, score, qkv, final):
    slots = jnp.arange(BLOCKS, dtype=jnp.int32)
    hit = (destination[None, :] == slots[:, None]) & (slots[None, :] < tally[0])
    source = jnp.sum(jnp.where(hit, slots[None, :], 0), axis=1)
    blocks, mixed, flags = layer(
        source,
        tally,
        softness,
        destination.reshape(1, BLOCKS),
        table.reshape(BLOCKS, BLOCK, C),
        order.reshape(BLOCKS, 1, BLOCK),
        entry,
        score,
        qkv,
        final,
    )
    settled = settle(softness, blocks, mixed, flags, entry, score, final)
    return settled.reshape(BLOCKS * BLOCK, C)


def solution(mesh):
    split = P(("grp", "pts"))
    rows = P(("grp", "pts"), None)
    return jax.shard_map(
        per_device,
        mesh=mesh,
        in_specs=(rows, split, split, rows, P(), P(), P(), P(), P()),
        out_specs=rows,
        check_vma=False,
    )
```

```python
import jax
import jax.numpy as jnp
from jax import lax
from jax.experimental import pallas as pl
from jax.experimental.pallas import tpu as pltpu
from jax.sharding import PartitionSpec as P

F32 = jnp.float32
BF16 = jnp.bfloat16
MESH = pl.DeviceIdType.MESH
LOG2E = 1.4426950408889634
NORM_EPS = 1e-05
SLICE_EPS = 1e-05
HIGHEST = lax.Precision.HIGHEST
NT = (((1,), (1,)), ((), ()))

C = 512
HEADS = 8
S = 256
HD = 64
BLOCK = 128
BLOCKS = 64
PEERS = 64
SIDE = 4
STEP_ROWS = 1024
STEP_BLOCKS = STEP_ROWS // BLOCK
STEPS = BLOCKS * BLOCK // STEP_ROWS
ACC_ROWS = HD + 16
MSG_ROWS = 24
VMEM_LIMIT = 60 << 20
SEND_STEP = 8
SEND_STEPS = 4
SEND_REDUCE = 0
SEND_BATCH = 9
EARLY = 2
PREPARED = 4


def whole(shape):
    return pl.BlockSpec(shape, lambda *_: (0,) * len(shape))


def normalize_rows(rows):
    values = rows.astype(F32)
    centred = values - jnp.mean(values, axis=-1, keepdims=True)
    spread = jnp.mean(centred * centred, axis=-1, keepdims=True)
    return (centred * lax.rsqrt(spread + NORM_EPS)).astype(BF16)


def head_weights(middle, score_ref, scale_ref, head):
    pair = middle[:, (head // 2) * 128 : (head // 2) * 128 + 128]
    scores = jnp.dot(pair, score_ref[head], preferred_element_type=F32)
    powered = jnp.exp2(scores * scale_ref[head])
    return (powered * (1.0 / jnp.sum(powered, axis=-1, keepdims=True))).astype(BF16)


def mix_tokens(tokens_ref, qkv_ref, mixed_ref):
    for head in range(HEADS):
        tokens = jnp.concatenate(
            [
                jnp.concatenate(
                    [tokens_ref[head * 8 + j, 0:8, :], tokens_ref[head * 8 + j, 8:16, :]], axis=1
                )
                for j in range(8)
            ],
            axis=0,
        )
        project = jnp.dot(qkv_ref[...], tokens, preferred_element_type=F32, precision=HIGHEST)
        queries = jnp.transpose(project[0:HD])
        scores = jnp.dot(
            queries, project[HD : 2 * HD], preferred_element_type=F32, precision=HIGHEST
        ) * (HD**-0.5)
        powered = jnp.exp(scores)
        attend = powered / jnp.sum(powered, axis=-1, keepdims=True)
        mixed = lax.dot_general(
            attend, project[2 * HD :], NT, preferred_element_type=F32, precision=HIGHEST
        )
        zeros = jnp.zeros_like(mixed)
        padded = [mixed, zeros] if head % 2 == 0 else [zeros, mixed]
        mixed_ref[head] = jnp.concatenate(padded, axis=1).astype(BF16)


def peer_at(me, i, sign):
    z, x, y = me // 16, (me // 4) % 4, me % 4
    a, b, c = i % 4, (i // 4) % 4, i // 16
    return (
        ((z + sign * a + 8) % SIDE) * 16
        + ((x + sign * (a + b) + 8) % SIDE) * 4
        + (y + sign * (a + c) + 8) % SIDE
    )


def finish_rows(block_rows, weights_of, mixed_ref, final_ref, flag_of, done_ref):
    spread = []
    for pair in range(HEADS // 2):
        first, second = weights_of(2 * pair), weights_of(2 * pair + 1)
        spread.append(
            (
                jnp.dot(first, mixed_ref[2 * pair], preferred_element_type=F32)
                + jnp.dot(second, mixed_ref[2 * pair + 1], preferred_element_type=F32)
            ).astype(BF16)
        )
    spread = jnp.concatenate(spread, axis=1)
    update = jnp.dot(spread, final_ref[...], preferred_element_type=F32)
    for j in range(block_rows.shape[0] // BLOCK):
        flag = flag_of(j)
        flag = jnp.concatenate([flag] * (C // 128), axis=1)
        part = slice(j * BLOCK, (j + 1) * BLOCK)
        done_ref[j] = ((block_rows[part].astype(F32) + update[part]) * flag).astype(BF16)


def prepare_scores(score_in_ref, softness_ref, score_ref, scale_ref):
    for head in range(HEADS):
        own, other = (head % 2) * HD, (1 - head % 2) * HD
        score_ref[head, own : own + HD, :] = score_in_ref[head]
        score_ref[head, other : other + HD, :] = jnp.zeros((HD, S), BF16)
        scale_ref[head] = LOG2E / jnp.full((1, S), softness_ref[head], F32)


def settle_kernel(
    softness_ref,
    blocks_hbm,
    mixed_ref,
    flags_ref,
    entry_ref,
    score_in_ref,
    final_ref,
    out_hbm,
    rows_ref,
    score_ref,
    scale_ref,
    load_sem,
    store_sem,
):
    me = lax.axis_index("pts")

    def load(step):
        part = pl.ds(step * STEP_BLOCKS, STEP_BLOCKS)
        return pltpu.make_async_copy(blocks_hbm.at[part], rows_ref.at[part], load_sem.at[step])

    def store(i):
        return pltpu.make_async_copy(
            rows_ref.at[i], out_hbm.at[peer_at(me, i, -1)], store_sem.at[i]
        )

    load(STEPS - 1).start()
    for step in range(STEPS - 1):
        load(step).start()
    prepare_scores(score_in_ref, softness_ref, score_ref, scale_ref)
    for step in range(STEPS - 1):
        load(step).wait()

        @pl.loop(step * STEP_BLOCKS, (step + 1) * STEP_BLOCKS)
        def _(i):
            store(i).start()

    load(STEPS - 1).wait()
    count = STEP_BLOCKS
    for half in range(1):
        first = (STEPS - 1) * STEP_BLOCKS + half * count
        block_rows = rows_ref[first : first + count].reshape(count * BLOCK, C)
        middle = jnp.dot(
            normalize_rows(block_rows), entry_ref[:, C:], preferred_element_type=F32
        ).astype(BF16)
        finish_rows(
            block_rows,
            lambda head: head_weights(middle, score_ref, scale_ref, head),
            mixed_ref,
            final_ref,
            lambda j: flags_ref[first + j, 2:3, :],
            rows_ref.at[pl.ds(first, count)],
        )
        @pl.loop(first, first + count)
        def _(i):
            store(i).start()

    @pl.loop(0, BLOCKS)
    def _(i):
        store(i).wait()


def settle(softness, blocks, mixed, flags, entry, score, final):
    smem = pl.BlockSpec(memory_space=pltpu.SMEM)
    vmem = pl.BlockSpec(memory_space=pltpu.VMEM)
    hbm = pl.BlockSpec(memory_space=pl.ANY)
    return pl.pallas_call(
        settle_kernel,
        name="settle",
        out_shape=jax.ShapeDtypeStruct((BLOCKS, BLOCK, C), BF16),
        in_specs=[smem, hbm, vmem, vmem, vmem, vmem, vmem],
        out_specs=hbm,
        scratch_shapes=[
            pltpu.VMEM((BLOCKS, BLOCK, C), BF16),
            pltpu.VMEM((HEADS, 2 * HD, S), BF16),
            pltpu.VMEM((HEADS, 1, S), F32),
            pltpu.SemaphoreType.DMA((STEPS,)),
            pltpu.SemaphoreType.DMA((BLOCKS,)),
        ],
        compiler_params=pltpu.CompilerParams(vmem_limit_bytes=VMEM_LIMIT),
    )(softness, blocks, mixed, flags, entry, score, final)


def layer_kernel(
    source_ref,
    tally_ref,
    softness_ref,
    destination_ref,
    table_hbm,
    order_ref,
    entry_ref,
    score_in_ref,
    qkv_in_ref,
    final_ref,
    out_hbm,
    mixed_hbm,
    flags_hbm,
    table_ref,
    outgoing_ref,
    arrived_ref,
    done_ref,
    weights_ref,
    feature_ref,
    score_ref,
    qkv_ref,
    scale_ref,
    flag_ref,
    acc_ref,
    msg_ref,
    got_ref,
    mine_ref,
    tokens_ref,
    mixed_ref,
    load_sem,
    store_sem,
    extra_sem,
    block_send,
    block_recv,
    sum_send,
    sum_recv,
    token_send,
    token_recv,
):
    me = lax.axis_index("pts")
    barrier = pltpu.get_barrier_semaphore()
    load = pltpu.make_async_copy(table_hbm, table_ref, load_sem)
    load.start()

    @pl.loop(1, PEERS)
    def _(i):
        pl.semaphore_signal(
            barrier, inc=1, device_id={"pts": peer_at(me, i, 1)}, device_id_type=MESH
        )

    def copy(src, dst, send, recv, i):
        return pltpu.make_async_remote_copy(
            src_ref=src,
            dst_ref=dst,
            send_sem=send.at[i],
            recv_sem=recv.at[i],
            device_id={"pts": peer_at(me, i, 1)},
            device_id_type=MESH,
        )

    def block_copy(i):
        return copy(outgoing_ref.at[i], arrived_ref.at[i], block_send, block_recv, i)

    def sum_copy(i):
        return copy(msg_ref.at[peer_at(me, i, 1)], got_ref.at[i], sum_send, sum_recv, i)

    def token_copy(i):
        return copy(mine_ref, tokens_ref.at[me], token_send, token_recv, i)

    def token_arrival(i):
        return copy(mine_ref, tokens_ref.at[peer_at(me, i, -1)], token_send, token_recv, i)

    columns = lax.broadcasted_iota(jnp.int32, (BLOCK, BLOCK), 1).astype(F32)

    def placed(i):
        b = source_ref[peer_at(me, i, 1)]
        wanted = jnp.broadcast_to(order_ref[b].astype(F32), (BLOCK, BLOCK))
        picking = (jnp.transpose(wanted) == columns).astype(F32).astype(BF16)
        return jnp.dot(picking, table_ref[b], preferred_element_type=F32).astype(BF16)

    def place(first, count):
        for j in range(count):
            outgoing_ref[first + j] = placed(first + j)

    def send(first, count):
        @pl.loop(first, first + count)
        def _(i):
            block_copy(i).start()

    feature_ref[...] = jnp.transpose(entry_ref[:, 0:C])
    qkv_ref[...] = jnp.transpose(qkv_in_ref[...].astype(F32))
    prepare_scores(score_in_ref, softness_ref, score_ref, scale_ref)
    slot = lax.broadcasted_iota(jnp.int32, (PEERS, BLOCKS), 1)
    peer = lax.broadcasted_iota(jnp.int32, (PEERS, BLOCKS), 0)
    hit = (destination_ref[...] == peer) & (slot < tally_ref[0])
    flag_ref[...] = jnp.broadcast_to(
        jnp.sum(hit.astype(F32), axis=1, keepdims=True), (PEERS, 128)
    )
    acc_ref[...] = jnp.zeros_like(acc_ref)
    load.wait()
    place(1, SEND_STEP)
    pl.semaphore_wait(barrier, PEERS - 1)

    @pl.loop(0, STEPS)
    def _(step):
        @pl.when(step < SEND_STEPS)
        def _():
            first = 1 + step * SEND_STEP
            send(first, SEND_STEP)
            place(first + SEND_STEP, SEND_STEP)

        part = table_ref[pl.ds(step * STEP_BLOCKS, STEP_BLOCKS)].reshape(STEP_ROWS, C)
        normed = normalize_rows(part)
        live = (
            lax.broadcasted_iota(jnp.int32, (1, STEP_ROWS), 1)
            < (tally_ref[0] - step * STEP_BLOCKS) * BLOCK
        ).astype(F32)
        features = lax.dot_general(feature_ref[...], normed, NT, preferred_element_type=F32)
        features = (features * live).astype(BF16)
        ones = jnp.broadcast_to(live, (16, STEP_ROWS)).astype(BF16)
        middle = jnp.dot(normed, entry_ref[:, C:], preferred_element_type=F32).astype(BF16)
        for head in range(HEADS):
            weights = head_weights(middle, score_ref, scale_ref, head)
            left = jnp.concatenate([features[head * HD : head * HD + HD], ones], axis=0)
            acc_ref[head] += jnp.dot(left, weights, preferred_element_type=F32)

    for p in range(PEERS):
        head, part = p // 8, (p % 8) * 8
        msg_ref[p, 0:8, :] = acc_ref[head, part : part + 8, 0:128]
        msg_ref[p, 8:16, :] = acc_ref[head, part : part + 8, 128:256]
        msg_ref[p, 16:17, :] = acc_ref[head, HD : HD + 1, 0:128]
        msg_ref[p, 17:18, :] = acc_ref[head, HD : HD + 1, 128:256]
        msg_ref[p, 18:19, :] = flag_ref[p : p + 1, :]
        msg_ref[p, 19:24, :] = jnp.zeros((5, 128), F32)

    sent = 1 + SEND_STEPS * SEND_STEP
    ready = sent + SEND_STEP
    arrived_ref[0] = placed(0)

    @pl.loop(1, PEERS)
    def _(i):
        sum_copy(i).start()

    if SEND_REDUCE:
        send(sent, SEND_REDUCE)
        sent += SEND_REDUCE
    place(ready, SEND_BATCH)
    ready += SEND_BATCH

    def wait_group(step):
        for j in range(STEP_BLOCKS):
            i = step * STEP_BLOCKS + j

            @pl.when(i > 0)
            def _():
                block_copy(i).wait_recv()

    def rows_of(step):
        return arrived_ref[pl.ds(step * STEP_BLOCKS, STEP_BLOCKS)].reshape(STEP_ROWS, C)

    def middle_of(step):
        return jnp.dot(
            normalize_rows(rows_of(step)), entry_ref[:, C:], preferred_element_type=F32
        ).astype(BF16)

    def prepare(first, last):
        @pl.loop(first, last)
        def _(step):
            wait_group(step)
            middle = middle_of(step)
            for head in range(HEADS):
                weights_ref[step, head] = head_weights(middle, score_ref, scale_ref, head)

    prepare(0, EARLY)
    got_ref[0] = msg_ref[me]

    def add(i, total):
        sum_copy(i).wait_recv()
        return total + got_ref[i]

    total = lax.fori_loop(1, PEERS, add, got_ref[0])
    mine_ref[0:8, :] = total[0:8] / (total[16:17] + SLICE_EPS)
    mine_ref[8:16, :] = total[8:16] / (total[17:18] + SLICE_EPS)
    tokens_ref[me] = mine_ref[...]

    @pl.loop(1, PEERS)
    def _(i):
        token_copy(i).start()

    while ready < PEERS:
        send(sent, ready - sent)
        sent = ready
        count = min(SEND_BATCH, PEERS - ready)
        place(ready, count)
        ready += count
    send(sent, PEERS - sent)
    prepare(EARLY, PREPARED)

    @pl.loop(1, PEERS)
    def _(i):
        token_arrival(i).wait_recv()

    mix_tokens(tokens_ref, qkv_ref, mixed_ref)

    share_mixed = pltpu.make_async_copy(mixed_ref, mixed_hbm, extra_sem.at[0])
    share_flags = pltpu.make_async_copy(
        got_ref.at[:, pl.ds(16, 8), :], flags_hbm, extra_sem.at[1]
    )
    share_flags.start()
    share_mixed.start()

    def store(step):
        return pltpu.make_async_copy(
            done_ref.at[step % 2],
            out_hbm.at[pl.ds(step * STEP_BLOCKS, STEP_BLOCKS)],
            store_sem.at[step % 2],
        )

    def finish(step, weights_of):
        @pl.when(step >= 2)
        def _():
            store(step - 2).wait()

        finish_rows(
            rows_of(step),
            weights_of,
            mixed_ref,
            final_ref,
            lambda j: got_ref[step * STEP_BLOCKS + j, 18:19, :],
            done_ref.at[step % 2],
        )
        store(step).start()

    @pl.loop(0, PREPARED)
    def _(step):
        finish(step, lambda head: weights_ref[step, head])

    @pl.loop(PREPARED, STEPS - 1)
    def _(step):
        wait_group(step)
        middle = middle_of(step)
        finish(step, lambda head: head_weights(middle, score_ref, scale_ref, head))

    wait_group(STEPS - 1)
    last = pl.ds((STEPS - 1) * STEP_BLOCKS, STEP_BLOCKS)
    rest = pltpu.make_async_copy(arrived_ref.at[last], out_hbm.at[last], extra_sem.at[2])
    rest.start()
    store(STEPS - 3).wait()
    store(STEPS - 2).wait()
    share_flags.wait()
    share_mixed.wait()

    @pl.loop(1, PEERS)
    def _(i):
        block_copy(i).wait_send()
        sum_copy(i).wait_send()
        token_copy(i).wait_send()

    rest.wait()


def layer(source, tally, softness, destination, table, order, entry, score, qkv, final):
    smem = pl.BlockSpec(memory_space=pltpu.SMEM)
    vmem = pl.BlockSpec(memory_space=pltpu.VMEM)
    hbm = pl.BlockSpec(memory_space=pl.ANY)
    dma = pltpu.SemaphoreType.DMA
    return pl.pallas_call(
        layer_kernel,
        name="layer",
        out_shape=(
            jax.ShapeDtypeStruct((BLOCKS, BLOCK, C), BF16),
            jax.ShapeDtypeStruct((HEADS, S, 128), BF16),
            jax.ShapeDtypeStruct((PEERS, 8, 128), F32),
        ),
        in_specs=[smem, smem, smem, vmem, hbm, vmem, vmem, vmem, vmem, vmem],
        out_specs=[hbm, hbm, hbm],
        scratch_shapes=[
            pltpu.VMEM((BLOCKS, BLOCK, C), BF16),
            pltpu.VMEM((BLOCKS, BLOCK, C), BF16),
            pltpu.VMEM((BLOCKS, BLOCK, C), BF16),
            pltpu.VMEM((2, STEP_BLOCKS, BLOCK, C), BF16),
            pltpu.VMEM((PREPARED, HEADS, STEP_ROWS, S), BF16),
            pltpu.VMEM((C, C), BF16),
            pltpu.VMEM((HEADS, 2 * HD, S), BF16),
            pltpu.VMEM((3 * HD, HD), F32),
            pltpu.VMEM((HEADS, 1, S), F32),
            pltpu.VMEM((PEERS, 128), F32),
            pltpu.VMEM((HEADS, ACC_ROWS, S), F32),
            pltpu.VMEM((PEERS, MSG_ROWS, 128), F32),
            pltpu.VMEM((PEERS, MSG_ROWS, 128), F32),
            pltpu.VMEM((16, 128), F32),
            pltpu.VMEM((PEERS, 16, 128), F32),
            pltpu.VMEM((HEADS, S, 128), BF16),
            dma,
            dma((2,)),
            dma((3,)),
            dma((PEERS,)),
            dma((PEERS,)),
            dma((PEERS,)),
            dma((PEERS,)),
            dma((PEERS,)),
            dma((PEERS,)),
        ],
        compiler_params=pltpu.CompilerParams(
            collective_id=1, has_side_effects=True, vmem_limit_bytes=VMEM_LIMIT
        ),
    )(source, tally, softness, destination, table, order, entry, score, qkv, final)


def per_device(table, tally, destination, order, softness, entry, score, qkv, final):
    slots = jnp.arange(BLOCKS, dtype=jnp.int32)
    hit = (destination[None, :] == slots[:, None]) & (slots[None, :] < tally[0])
    source = jnp.sum(jnp.where(hit, slots[None, :], 0), axis=1)
    blocks, mixed, flags = layer(
        source,
        tally,
        softness,
        destination.reshape(1, BLOCKS),
        table.reshape(BLOCKS, BLOCK, C),
        order.reshape(BLOCKS, 1, BLOCK),
        entry,
        score,
        qkv,
        final,
    )
    settled = settle(softness, blocks, mixed, flags, entry, score, final)
    return settled.reshape(BLOCKS * BLOCK, C)


def solution(mesh):
    split = P(("grp", "pts"))
    rows = P(("grp", "pts"), None)
    return jax.shard_map(
        per_device,
        mesh=mesh,
        in_specs=(rows, split, split, rows, P(), P(), P(), P(), P()),
        out_specs=rows,
        check_vma=False,
    )
```
